128 devices in a mesh: fsdp: 4 (over y_lo, core), ctx: 32 (over z, y_hi, x).
Axes of the slice: x: 4, y: 4 (y_hi: 2, y_lo: 2; y = y_hi * 2 + y_lo), z: 4, core: 2. Of those that a mesh axis runs over, the one named last changes fastest.
Arguments:
- query_proj: bfloat16 [4, 4096, 4096], P('fsdp', 'ctx'), may hold values from -10 to 10
- key_proj: bfloat16 [4, 4096, 4096], P('fsdp', 'ctx'), may hold values from -10 to 10
- value_proj: bfloat16 [4, 4096, 4096], P('fsdp', 'ctx'), may hold values from -12 to 12
- modality: int32 [4, 4096], P('fsdp', 'ctx'), may hold values from 0 to 1, as said below
- out_weight: bfloat16 [2, 4096, 2048], P(None, ('fsdp', 'ctx')), may hold values from -0.09375 to 0.09375
- grad_projected: bfloat16 [4, 4096, 2048], P('fsdp', 'ctx'), may hold values from -6 to 6
Outputs:
- projected: bfloat16 [4, 4096, 2048], P('fsdp', 'ctx')
- grad_query: bfloat16 [4, 4096, 4096], P('fsdp', 'ctx')
- grad_key: bfloat16 [4, 4096, 4096], P('fsdp', 'ctx')
- grad_value: bfloat16 [4, 4096, 4096], P('fsdp', 'ctx')
The draws below stay inside these ranges and needn't reach their ends.
Inputs may be any that keep to these rules, and one draw needn't show every extreme that they name: `modality`: each sequence holds exactly two image spans of 1024 positions each, one starting within the first half and lying in the first half, the other lying in the second half; all other positions are text, so exactly half of each sequence's positions are image.
All inputs are finite; a program needn't handle non-finite values.
Results may differ from the reference program's by a relative error of at most 0.012.
The reference program's roundings to bfloat16 on the way count: a program that leaves them out, or rounds other values in their place, can miss the bound.
Values may be sent and summed in bfloat16 or wider, within the bound.
No kernel may reach another device: no remote copies, remote signals or barrier semaphores. Data moves between devices by JAX's collectives and lax.ppermute only.
A program may use at most 320 MiB of HBM per device.

```python
import jax
import jax.numpy as jnp
from jax import lax

HEAD_COUNT = 32
HEAD_SIZE = 128
OUT_WIDTH = 2048
LENGTH = 4096
IMAGE_SPAN = 1024
SEQUENCES = 4


def base_draw(key, offset_tag):
    folded = jax.random.fold_in(key, offset_tag)
    extent = (SEQUENCES, LENGTH, HEAD_COUNT * HEAD_SIZE)
    return jnp.clip(1.3 * jax.random.normal(folded, extent, jnp.float32), -6.0, 6.0)


def draw_query_proj(key, part):
    values = base_draw(key, 11)
    return values.astype(jnp.bfloat16)


def draw_key_proj(key, part):
    values = base_draw(key, 23)
    return values.astype(jnp.bfloat16)


def draw_modality(key, part):
    folded = jax.random.fold_in(key, 5)
    first_key, second_key = jax.random.split(folded, 2)
    first_start = jax.random.randint(first_key, (SEQUENCES,), 0, LENGTH // 2 - IMAGE_SPAN + 1)
    second_start = jax.random.randint(second_key, (SEQUENCES,), LENGTH // 2, LENGTH - IMAGE_SPAN + 1)
    places = jnp.arange(LENGTH)[None, :]
    inside_first = (places >= first_start[:, None]) & (places < first_start[:, None] + IMAGE_SPAN)
    inside_second = (places >= second_start[:, None]) & (places < second_start[:, None] + IMAGE_SPAN)
    return (inside_first | inside_second).astype(jnp.int32)


def block_scale(stream_key, shape, cuts, smallest, top_value):
    gain = 1.0
    for position, blocks in cuts:
        heights = jax.random.uniform(jax.random.fold_in(jax.random.fold_in(stream_key, 6), position), (blocks,), jnp.float32, smallest / len(cuts), top_value / len(cuts))
        gain = gain * jnp.repeat(jnp.exp(heights), shape[position] // blocks).reshape((-1,) + (1,) * (len(shape) - 1 - position))
    return gain


def centred(key, dims, width, reach, cuts=(), kind=jnp.bfloat16):
    values = width * jax.random.normal(key, dims, jnp.float32)
    if cuts:
        values = values * block_scale(key, dims, cuts, -0.22, 0.18)
    return jnp.clip(values, -reach, reach).astype(kind)


def setup_inputs(seed: int = 0) -> dict:
    key_of = jax.random.split(jax.random.key(seed), 7)
    return {
        "query_proj": draw_query_proj(jax.random.fold_in(key_of[6], 71), 0),
        "key_proj": draw_key_proj(jax.random.fold_in(key_of[6], 71), 0),
        "value_proj": centred(key_of[2], (SEQUENCES, LENGTH, HEAD_COUNT * HEAD_SIZE), 2.0, 12.0, ((0, 4), (1, 32))),
        "modality": draw_modality(jax.random.fold_in(key_of[6], 71), 0),
        "out_weight": centred(key_of[4], (2, HEAD_COUNT * HEAD_SIZE, OUT_WIDTH), (HEAD_COUNT * HEAD_SIZE) ** -0.5, 0.09375, ((1, 128),)),
        "grad_projected": centred(key_of[5], (SEQUENCES, LENGTH, OUT_WIDTH), 1.0, 6.0, ((0, 4), (1, 32))),
    }


def block_count(length):
    return max(1, min(8, length // 512))


def rounded(matrix):
    return lax.optimization_barrier(matrix.astype(jnp.bfloat16)).astype(jnp.float32)


def probabilities(query_block, key_prefix, offset):
    scaling = query_block.shape[-1] ** -0.5
    scores = jnp.einsum("qhd,khd->hqk", query_block.astype(jnp.float32), key_prefix.astype(jnp.float32)) * scaling
    query_places = offset + jnp.arange(query_block.shape[0])
    key_places = jnp.arange(key_prefix.shape[0])
    scores = jnp.where(key_places[None, None, :] <= query_places[None, :, None], scores, -jnp.inf)
    highest = jnp.max(scores, axis=-1, keepdims=True)
    raised = jnp.exp(scores - highest)
    return raised / jnp.sum(raised, axis=-1, keepdims=True)


def attend_forward(queries, keys_all, values_all):
    length = queries.shape[0]
    block_rows = length // block_count(length)
    pieces = []
    for block_index in range(length // block_rows):
        offset = block_index * block_rows
        finish = offset + block_rows
        weights = probabilities(queries[offset:finish], keys_all[:finish], offset)
        output = jnp.einsum("hqk,khd->qhd", rounded(weights), values_all[:finish].astype(jnp.float32))
        pieces.append(output.astype(jnp.bfloat16))
    return jnp.concatenate(pieces, axis=0)


def attend_backward(queries, keys_all, values_all, attention, grad_attention):
    length = queries.shape[0]
    block_rows = length // block_count(length)
    scaling = queries.shape[-1] ** -0.5
    grad_keys = jnp.zeros(queries.shape, jnp.float32)
    grad_values = jnp.zeros(queries.shape, jnp.float32)
    query_pieces = []
    for block_index in range(length // block_rows):
        offset = block_index * block_rows
        finish = offset + block_rows
        query_block = queries[offset:finish]
        weights = probabilities(query_block, keys_all[:finish], offset)
        grad_block = grad_attention[offset:finish].astype(jnp.float32)
        attn_block = attention[offset:finish].astype(jnp.float32)
        grad_values = grad_values.at[:finish].add(jnp.einsum("hqk,qhd->khd", rounded(weights), grad_block))
        grad_weights = jnp.einsum("qhd,khd->hqk", grad_block, values_all[:finish].astype(jnp.float32))
        row_delta = jnp.sum(grad_block * attn_block, axis=-1).T[:, :, None]
        grad_scores = rounded(weights * (grad_weights - row_delta) * scaling)
        query_pieces.append(jnp.einsum("hqk,khd->qhd", grad_scores, keys_all[:finish].astype(jnp.float32)).astype(jnp.bfloat16))
        grad_keys = grad_keys.at[:finish].add(jnp.einsum("hqk,qhd->khd", grad_scores, query_block.astype(jnp.float32)))
    return jnp.concatenate(query_pieces, axis=0), grad_keys.astype(jnp.bfloat16), grad_values.astype(jnp.bfloat16)


def reference(query_proj, key_proj, value_proj, modality, out_weight, grad_projected):
    def per_sequence(inputs):
        queries, keys_all, values_all, modal_ids, upstream = inputs
        shaped = (LENGTH, HEAD_COUNT, HEAD_SIZE)
        inner_width = HEAD_COUNT * HEAD_SIZE
        queries = queries.reshape(shaped)
        keys_all = keys_all.reshape(shaped)
        values_all = values_all.reshape(shaped)
        attention = attend_forward(queries, keys_all, values_all)
        flat = attention.reshape(LENGTH, inner_width)
        is_image = (modal_ids == 1)[:, None]
        text_out = jnp.dot(flat, out_weight[0], preferred_element_type=jnp.float32)
        image_out = jnp.dot(flat, out_weight[1], preferred_element_type=jnp.float32)
        result = jnp.where(is_image, image_out, text_out).astype(jnp.bfloat16)
        text_back = jnp.dot(upstream, out_weight[0].T, preferred_element_type=jnp.float32)
        image_back = jnp.dot(upstream, out_weight[1].T, preferred_element_type=jnp.float32)
        grad_attention = jnp.where(is_image, image_back, text_back).astype(jnp.bfloat16).reshape(shaped)
        grad_q, grad_k, grad_v = attend_backward(queries, keys_all, values_all, attention, grad_attention)
        return result, grad_q.reshape(LENGTH, inner_width), grad_k.reshape(LENGTH, inner_width), grad_v.reshape(LENGTH, inner_width)

    projected, grad_query, grad_key, grad_value = lax.map(per_sequence, (query_proj, key_proj, value_proj, modality, grad_projected))
    return (projected, grad_query, grad_key, grad_value)
```

```python
import functools, math
import jax, jax.numpy as jnp
from jax import lax
from jax.experimental import pallas as pl
from jax.experimental.pallas import tpu as pltpu
from jax.sharding import PartitionSpec as P

HEAD_SIZE = 128
LOG2E = math.log2(math.e)
NT = (((1,), (1,)), ((), ()))
TN = (((0,), (0,)), ((), ()))
VMEM_LIMIT = 56 * 1024 * 1024
FWD_ROWS = 1024
BWD_ROWS = 1024


def mm(a, b, dims=(((1,), (0,)), ((), ()))):
    return lax.dot_general(a, b, dims, preferred_element_type=jnp.float32)


def fwd_kernel(qkv_ref, out_ref, lse_ref, s_ref, *, rows):
    blocks, _, step, _ = qkv_ref.shape
    per = rows // step
    count = blocks // per
    factor = HEAD_SIZE**-0.5 * LOG2E

    def get(which, index):
        return qkv_ref[pl.ds(index * per, per), which].reshape(rows, HEAD_SIZE)

    def query_block(i, _):
        query = get(0, i)

        def scores(j, top):
            s = mm(query, get(1, j), NT)
            s_ref[j] = s
            for c in range(0, rows, HEAD_SIZE):
                top = jnp.maximum(top, s[:, c : c + HEAD_SIZE])
            return top

        top = lax.fori_loop(0, i, scores, jnp.full((rows, HEAD_SIZE), -jnp.inf, jnp.float32))
        s = mm(query, get(1, i), NT)
        keep = lax.broadcasted_iota(jnp.int32, s.shape, 1) <= lax.broadcasted_iota(
            jnp.int32, s.shape, 0
        )
        s = jnp.where(keep, s, -jnp.inf)
        s_ref[i] = s
        for c in range(0, rows, HEAD_SIZE):
            top = jnp.maximum(top, s[:, c : c + HEAD_SIZE])
        high = jnp.max(top, axis=1, keepdims=True) * factor

        def values(j, carry):
            total, acc = carry
            p = jnp.exp2(s_ref[j] * factor - high)
            for c in range(0, rows, HEAD_SIZE):
                total = total + p[:, c : c + HEAD_SIZE]
            return total, acc + mm(p.astype(jnp.bfloat16), get(2, j))

        zero = jnp.zeros((rows, HEAD_SIZE), jnp.float32)
        total, acc = lax.fori_loop(0, i + 1, values, (zero, zero))
        total = jnp.sum(total, axis=1, keepdims=True)
        out = (acc / total).astype(jnp.bfloat16)
        out_ref[pl.ds(i * per, per)] = out.reshape(per, step, HEAD_SIZE)
        lse = jnp.broadcast_to(high + jnp.log2(total), (rows, HEAD_SIZE))
        lse_ref[pl.ds(i, 1)] = lse.T[0:1].reshape(1, 1, rows)
        return 0

    lax.fori_loop(0, count, query_block, 0)


def attend_forward(qkv, rows=512):
    blocks, _, step, _ = qkv.shape
    length = blocks * step
    return pl.pallas_call(
        functools.partial(fwd_kernel, rows=rows),
        out_shape=(
            jax.ShapeDtypeStruct((blocks, step, HEAD_SIZE), jnp.bfloat16),
            jax.ShapeDtypeStruct((length // rows, 1, rows), jnp.float32),
        ),
        in_specs=[pl.BlockSpec(memory_space=pltpu.VMEM)],
        out_specs=[pl.BlockSpec(memory_space=pltpu.VMEM)] * 2,
        scratch_shapes=[pltpu.VMEM((length // rows, rows, rows), jnp.float32)],
        compiler_params=pltpu.CompilerParams(vmem_limit_bytes=VMEM_LIMIT),
        cost_estimate=pl.CostEstimate(
            flops=2 * length * length * HEAD_SIZE,
            bytes_accessed=8 * length * HEAD_SIZE,
            transcendentals=length * length // 2,
        ),
        name="attend_forward",
    )(qkv)


def bwd_kernel(qkv_ref, out_ref, lse_ref, grad_ref, res_ref, dq_ref, dk_ref, dv_ref, *, rows):
    blocks, _, step, _ = qkv_ref.shape
    per = rows // step
    count = blocks // per
    scale = HEAD_SIZE**-0.5
    factor = scale * LOG2E

    def get(which, index):
        return qkv_ref[pl.ds(index * per, per), which].reshape(rows, HEAD_SIZE)

    dk_ref[...] = jnp.zeros_like(dk_ref)
    dv_ref[...] = jnp.zeros_like(dv_ref)

    def query_block(i, _):
        query = get(0, i)
        grad = grad_ref[pl.ds(i * per, per)].reshape(rows, HEAD_SIZE)
        attn = out_ref[pl.ds(i * per, per)].reshape(rows, HEAD_SIZE)
        prod = grad.astype(jnp.float32) * attn.astype(jnp.float32)
        delta = jnp.sum(prod.T, axis=0, keepdims=True)
        lse = lse_ref[i]
        dq_ref[...] = jnp.zeros_like(dq_ref)

        def key_block(j, diagonal):
            key = get(1, j)
            at = pl.ds(j * rows, rows)
            p = jnp.exp2(mm(key, query, NT) * factor - lse)
            if diagonal:
                keep = lax.broadcasted_iota(jnp.int32, p.shape, 0) <= lax.broadcasted_iota(
                    jnp.int32, p.shape, 1
                )
                p = jnp.where(keep, p, 0.0)
            dv_ref[at] += mm(p.astype(jnp.bfloat16), grad)
            ds = (p * (mm(get(2, j), grad, NT) - delta) * scale).astype(jnp.bfloat16)
            dk_ref[at] += mm(ds, query)
            dq_ref[...] += mm(ds, key, TN)

        def body(j, _):
            key_block(j, False)
            return 0

        lax.fori_loop(0, i, body, 0)
        key_block(i, True)
        res_ref[pl.ds(i * per, per), 0] = (
            dq_ref[...].astype(jnp.bfloat16).reshape(per, step, HEAD_SIZE)
        )
        return 0

    lax.fori_loop(0, count, query_block, 0)
    res_ref[:, 1] = dk_ref[...].astype(jnp.bfloat16).reshape(blocks, step, HEAD_SIZE)
    res_ref[:, 2] = dv_ref[...].astype(jnp.bfloat16).reshape(blocks, step, HEAD_SIZE)


def attend_backward(qkv, out, lse, grad, rows=512):
    blocks, _, step, _ = qkv.shape
    length = blocks * step
    lse = lse.reshape(length // rows, 1, rows)
    return pl.pallas_call(
        functools.partial(bwd_kernel, rows=rows),
        out_shape=jax.ShapeDtypeStruct((blocks, 3, step, HEAD_SIZE), jnp.bfloat16),
        in_specs=[pl.BlockSpec(memory_space=pltpu.VMEM)] * 4,
        out_specs=pl.BlockSpec(memory_space=pltpu.VMEM),
        scratch_shapes=[
            pltpu.VMEM((rows, HEAD_SIZE), jnp.float32),
            pltpu.VMEM((length, HEAD_SIZE), jnp.float32),
            pltpu.VMEM((length, HEAD_SIZE), jnp.float32),
        ],
        compiler_params=pltpu.CompilerParams(vmem_limit_bytes=VMEM_LIMIT),
        cost_estimate=pl.CostEstimate(
            flops=5 * length * length * HEAD_SIZE,
            bytes_accessed=16 * length * HEAD_SIZE,
            transcendentals=length * length // 2,
        ),
        name="attend_backward",
    )(qkv, out, lse, grad)


def pack_kernel(q_ref, k_ref, v_ref, out_ref):
    for h in range(out_ref.shape[0]):
        at = slice(h * HEAD_SIZE, (h + 1) * HEAD_SIZE)
        for w, ref in enumerate((q_ref, k_ref, v_ref)):
            out_ref[h, w] = ref[:, at]


def pack_heads(arrays, group=4):
    step, width = arrays[0].shape
    heads = width // HEAD_SIZE
    flat = pl.BlockSpec((step, group * HEAD_SIZE), lambda g: (0, g))
    return pl.pallas_call(
        pack_kernel,
        grid=(heads // group,),
        out_shape=jax.ShapeDtypeStruct((heads, 3, step, HEAD_SIZE), jnp.bfloat16),
        in_specs=[flat] * 3,
        out_specs=pl.BlockSpec((group, 3, step, HEAD_SIZE), lambda g: (g, 0, 0, 0)),
        name="pack_heads",
    )(*arrays)


def unpack_kernel(in_ref, q_ref, k_ref, v_ref):
    for h in range(in_ref.shape[0]):
        at = slice(h * HEAD_SIZE, (h + 1) * HEAD_SIZE)
        for w, ref in enumerate((q_ref, k_ref, v_ref)):
            ref[:, at] = in_ref[h, w]


def unpack_heads(stacked, group=4):
    heads, _, step, _ = stacked.shape
    flat = pl.BlockSpec((step, group * HEAD_SIZE), lambda g: (0, g))
    return pl.pallas_call(
        unpack_kernel,
        grid=(heads // group,),
        out_shape=[jax.ShapeDtypeStruct((step, heads * HEAD_SIZE), jnp.bfloat16)] * 3,
        in_specs=[pl.BlockSpec((group, 3, step, HEAD_SIZE), lambda g: (g, 0, 0, 0))],
        out_specs=[flat] * 3,
        name="unpack_heads",
    )(stacked)


def weight_pair(w_ref, kind):
    pair = [w_ref[0, :, y, kind].reshape(HEAD_SIZE, w_ref.shape[-1]) for y in range(2)]
    return jnp.concatenate(pair, axis=0)


def project_back_kernel(pay_ref, w_ref, out_ref):
    groups, step, _ = pay_ref.shape
    width = w_ref.shape[-1]
    upstream = pay_ref[:, :, :width].reshape(groups * step, width)
    text = mm(upstream, weight_pair(w_ref, 0), NT)
    image = mm(upstream, weight_pair(w_ref, 1), NT)
    for b in range(groups):
        mask = pay_ref[b, :, width:].astype(jnp.float32) > 0.5
        rows = slice(b * step, (b + 1) * step)
        for y in range(2):
            at = slice(y * HEAD_SIZE, (y + 1) * HEAD_SIZE)
            out_ref[b, y] = jnp.where(mask, image[rows, at], text[rows, at]).astype(jnp.bfloat16)


def weight_spec(weights):
    return pl.BlockSpec((1, *weights.shape[1:]), lambda z: (z, 0, 0, 0, 0, 0))


def project_back(payload, weights):
    groups, step, _ = payload.shape
    return pl.pallas_call(
        project_back_kernel,
        grid=(weights.shape[0],),
        out_shape=jax.ShapeDtypeStruct(
            (groups, 2 * weights.shape[0], step, HEAD_SIZE), jnp.bfloat16
        ),
        in_specs=[pl.BlockSpec(memory_space=pltpu.VMEM), weight_spec(weights)],
        out_specs=pl.BlockSpec((groups, 2, step, HEAD_SIZE), lambda z: (0, z, 0, 0)),
        compiler_params=pltpu.CompilerParams(vmem_limit_bytes=VMEM_LIMIT),
        cost_estimate=pl.CostEstimate(
            flops=2 * groups * step * weights.size, bytes_accessed=2 * weights.size, transcendentals=0
        ),
        name="project_back",
    )(payload, weights)


def project_kernel(attn_ref, pay_ref, w_ref, out_ref, acc_ref):
    groups, _, step, _ = attn_ref.shape
    width = w_ref.shape[-1]

    @pl.when(pl.program_id(0) == 0)
    def _():
        acc_ref[...] = jnp.zeros_like(acc_ref)

    text, image = [], []
    for b in range(groups):
        mask = pay_ref[b, :, width:].astype(jnp.float32) > 0.5
        parts = [attn_ref[b, y].astype(jnp.float32) for y in range(2)]
        text.append(jnp.concatenate([jnp.where(mask, 0.0, p) for p in parts], axis=1))
        image.append(jnp.concatenate([jnp.where(mask, p, 0.0) for p in parts], axis=1))
    text = jnp.concatenate(text, axis=0).astype(jnp.bfloat16)
    image = jnp.concatenate(image, axis=0).astype(jnp.bfloat16)
    acc_ref[...] += mm(text, weight_pair(w_ref, 0)) + mm(image, weight_pair(w_ref, 1))

    @pl.when(pl.program_id(0) == pl.num_programs(0) - 1)
    def _():
        out_ref[...] = acc_ref[...].astype(out_ref.dtype).reshape(out_ref.shape)


def project(attn, payload, weights):
    groups, _, step, _ = attn.shape
    width = weights.shape[-1]
    return pl.pallas_call(
        project_kernel,
        grid=(weights.shape[0],),
        out_shape=jax.ShapeDtypeStruct((groups, step, width), jnp.bfloat16),
        in_specs=[
            pl.BlockSpec((groups, 2, step, HEAD_SIZE), lambda z: (0, z, 0, 0)),
            pl.BlockSpec(memory_space=pltpu.VMEM),
            weight_spec(weights),
        ],
        out_specs=pl.BlockSpec((groups, step, width), lambda z: (0, 0, 0)),
        scratch_shapes=[pltpu.VMEM((groups * step, width), jnp.float32)],
        compiler_params=pltpu.CompilerParams(vmem_limit_bytes=VMEM_LIMIT),
        cost_estimate=pl.CostEstimate(
            flops=2 * groups * step * weights.size, bytes_accessed=2 * weights.size, transcendentals=0
        ),
        name="project",
    )(attn, payload, weights)


CTX = ("z", "yh", "x")


def exchange(blocks, axis):
    return lax.all_to_all(blocks, axis, split_axis=0, concat_axis=0, tiled=True)


def per_device(query_proj, key_proj, value_proj, modality, out_weight, grad_projected):
    groups = lax.axis_size("fsdp")
    step, inner = query_proj.shape[1:]
    heads = inner // HEAD_SIZE
    quarter = heads // groups
    pair = lax.all_gather(out_weight, "yh", axis=0)
    weights = lax.all_gather(pair, ("z", "x"), axis=0)
    weights = weights.reshape(lax.axis_size("z"), lax.axis_size("x"), *pair.shape)

    qkv = exchange(pack_heads((query_proj[0], key_proj[0], value_proj[0])), CTX)
    kind = jnp.broadcast_to(modality[0][:, None], (step, HEAD_SIZE)).astype(jnp.bfloat16)
    payload = jnp.concatenate([grad_projected[0], kind], axis=1)
    payload = exchange(jnp.broadcast_to(payload, (groups, *payload.shape)), "fsdp")

    attention, lse = attend_forward(qkv, FWD_ROWS)
    attn_rows = exchange(attention, CTX).reshape(groups, quarter, step, HEAD_SIZE)
    attn_rows = exchange(attn_rows, "fsdp")

    grad_rows = exchange(project_back(payload, weights), "fsdp")
    grad_heads = exchange(grad_rows.reshape(heads, step, HEAD_SIZE), CTX)
    partial = exchange(project(attn_rows, payload, weights), "fsdp")
    total = partial[0].astype(jnp.float32)
    for f in range(1, groups):
        total = total + partial[f].astype(jnp.float32)
    projected = total.astype(jnp.bfloat16)[None]

    grads = attend_backward(qkv, attention, lse, grad_heads, BWD_ROWS)
    grad_query, grad_key, grad_value = unpack_heads(exchange(grads, CTX))
    return projected, grad_query[None], grad_key[None], grad_value[None]


def solution(mesh):
    grid = jax.sharding.Mesh(mesh.devices.reshape(-1, 4, 2, 4), ("fsdp", *CTX))
    rows = P("fsdp", CTX, None)
    placed = (rows, rows, rows, P("fsdp", CTX), P(None, ("fsdp", *CTX), None), rows)
    return jax.shard_map(
        per_device,
        mesh=grid,
        in_specs=placed,
        out_specs=(rows,) * 4,
        check_vma=False,
    )
```

```python
import functools, math
import jax, jax.numpy as jnp
from jax import lax
from jax.experimental import pallas as pl
from jax.experimental.pallas import tpu as pltpu
from jax.sharding import PartitionSpec as P

HEAD_SIZE = 128
LOG2E = math.log2(math.e)
NT = (((1,), (1,)), ((), ()))
TN = (((0,), (0,)), ((), ()))
VMEM_LIMIT = 56 * 1024 * 1024
FWD_ROWS = 1024
BWD_ROWS = 1024
KIND_ROWS = 16
PACK = 2


def mm(a, b, dims=(((1,), (0,)), ((), ()))):
    return lax.dot_general(a, b, dims, preferred_element_type=jnp.float32)


def visible(shape, key_dim, shift):
    keys = lax.broadcasted_iota(jnp.int32, shape, key_dim)
    return keys + shift <= lax.broadcasted_iota(jnp.int32, shape, 1 - key_dim)


def fwd_kernel(me_ref, qkv_ref, out_ref, own_ref, other_ref, lse_ref, s_ref, *, rows):
    blocks = qkv_ref.shape[0]
    step = HEAD_SIZE
    per = rows // step
    count = blocks // per
    half = rows // 2
    factor = HEAD_SIZE**-0.5 * LOG2E

    def get(which, first, size):
        part = qkv_ref[pl.ds(first, size // step), which * step : (which + 1) * step]
        return part.reshape(size, HEAD_SIZE)

    def fold(op, start, s):
        for c in range(0, s.shape[1], HEAD_SIZE):
            start = op(start, s[:, c : c + HEAD_SIZE])
        return start

    def query_block(i, _):
        query = get(0, i * per, rows)

        def scores(j, top):
            s = mm(query, get(1, j * per, rows), NT)
            s_ref[j] = s
            return fold(jnp.maximum, top, s)

        top = lax.fori_loop(0, i, scores, jnp.full((rows, HEAD_SIZE), -jnp.inf, jnp.float32))
        highs = []
        for part in range(2):
            size = half * (part + 1)
            at = slice(part * half, (part + 1) * half)
            s = mm(query[at], get(1, i * per, size), NT)
            s = jnp.where(visible(s.shape, 1, -part * half), s, -jnp.inf)
            s_ref[i, at, :size] = s
            highs.append(jnp.max(fold(jnp.maximum, top[at], s), axis=1, keepdims=True) * factor)
        high = jnp.concatenate(highs, axis=0)

        def values(j, carry):
            total, acc = carry
            p = jnp.exp2(s_ref[j] * factor - high)
            total = fold(jnp.add, total, p)
            return total, acc + mm(p.astype(jnp.bfloat16), get(2, j * per, rows))

        zero = jnp.zeros((rows, HEAD_SIZE), jnp.float32)
        totals, accs = lax.fori_loop(0, i, values, (zero, zero))
        for part in range(2):
            size = half * (part + 1)
            at = slice(part * half, (part + 1) * half)
            p = jnp.exp2(s_ref[i, at, :size] * factor - highs[part])
            total = jnp.sum(fold(jnp.add, totals[at], p), axis=1, keepdims=True)
            acc = accs[at] + mm(p.astype(jnp.bfloat16), get(2, i * per, size))
            out = (acc / total).astype(jnp.bfloat16)
            out_ref[pl.ds(i * per + part * per // 2, per // 2)] = out.reshape(-1, step, HEAD_SIZE)
            lse = jnp.broadcast_to(highs[part] + jnp.log2(total), (half, HEAD_SIZE))
            lse_ref[i, :, at] = lse.T[0:1]
        return 0

    lax.fori_loop(0, count, query_block, 0)
    me = me_ref[0]
    half = blocks // 8
    for z in range(4):
        own_ref[z * half : (z + 1) * half] = out_ref[pl.ds((2 * z + me) * half, half)]
        other_ref[z * half : (z + 1) * half] = out_ref[pl.ds((2 * z + 1 - me) * half, half)]


def attend_forward(me, qkv, rows):
    blocks, step = qkv.shape[0], HEAD_SIZE
    length = blocks * step
    return pl.pallas_call(
        functools.partial(fwd_kernel, rows=rows),
        out_shape=(
            jax.ShapeDtypeStruct((blocks, step, HEAD_SIZE), jnp.bfloat16),
            jax.ShapeDtypeStruct((blocks // 2, step, HEAD_SIZE), jnp.bfloat16),
            jax.ShapeDtypeStruct((blocks // 2, step, HEAD_SIZE), jnp.bfloat16),
            jax.ShapeDtypeStruct((length // rows, 1, rows), jnp.float32),
        ),
        in_specs=[
            pl.BlockSpec(memory_space=pltpu.SMEM),
            pl.BlockSpec(memory_space=pltpu.VMEM),
        ],
        out_specs=[pl.BlockSpec(memory_space=pltpu.VMEM)] * 4,
        scratch_shapes=[pltpu.VMEM((length // rows, rows, rows), jnp.float32)],
        compiler_params=pltpu.CompilerParams(vmem_limit_bytes=VMEM_LIMIT),
        cost_estimate=pl.CostEstimate(
            flops=12 * length * length * HEAD_SIZE,
            bytes_accessed=8 * length * HEAD_SIZE,
            transcendentals=length * length // 2,
        ),
        name="attend_forward",
    )(me, qkv)


def bwd_kernel(
    me_ref, qkv_ref, out_ref, lse_ref, own_ref, other_ref, res_ref, grad_ref, dq_ref, dk_ref, dv_ref, *, rows
):
    blocks = qkv_ref.shape[0]
    step = HEAD_SIZE
    per = rows // step
    count = blocks // per
    scale = HEAD_SIZE**-0.5
    factor = scale * LOG2E

    def get(which, first, size):
        part = qkv_ref[pl.ds(first, size // step), which * step : (which + 1) * step]
        return part.reshape(size, HEAD_SIZE)

    me = me_ref[0]
    half = blocks // 8
    for z in range(4):
        grad_ref[pl.ds((2 * z + me) * half, half)] = own_ref[z * half : (z + 1) * half]
        grad_ref[pl.ds((2 * z + 1 - me) * half, half)] = other_ref[z * half : (z + 1) * half]
    dk_ref[...] = jnp.zeros_like(dk_ref)
    dv_ref[...] = jnp.zeros_like(dv_ref)

    def query_block(i, _):
        query = get(0, i * per, rows)
        grad = grad_ref[pl.ds(i * per, per)].reshape(rows, HEAD_SIZE)
        attn = out_ref[pl.ds(i * per, per)].reshape(rows, HEAD_SIZE)
        prod = grad.astype(jnp.float32) * attn.astype(jnp.float32)
        delta = jnp.sum(prod.T, axis=0, keepdims=True)
        lse = lse_ref[i]
        dq_ref[...] = jnp.zeros_like(dq_ref)

        def key_block(j, size, at, shift=None):
            key = get(1, j * per, size)
            to = pl.ds(j * rows, size)
            p = jnp.exp2(mm(key, query[at], NT) * factor - lse[:, at])
            if shift is not None:
                p = jnp.where(visible(p.shape, 0, shift), p, 0.0)
            dv_ref[to] += mm(p.astype(jnp.bfloat16), grad[at])
            ds = p * (mm(get(2, j * per, size), grad[at], NT) - delta[:, at]) * scale
            ds = ds.astype(jnp.bfloat16)
            dk_ref[to] += mm(ds, query[at])
            dq_ref[at] += mm(ds, key, TN)

        def body(j, _):
            key_block(j, rows, slice(0, rows))
            return 0

        lax.fori_loop(0, i, body, 0)
        middle = rows // 2
        key_block(i, middle, slice(0, middle), 0)
        key_block(i, rows, slice(middle, rows), -middle)
        done = dq_ref[...].astype(jnp.bfloat16).reshape(per, step, HEAD_SIZE)
        res_ref[pl.ds(i * per, per), 0] = done
        return 0

    lax.fori_loop(0, count, query_block, 0)
    res_ref[:, 1] = dk_ref[...].astype(jnp.bfloat16).reshape(blocks, step, HEAD_SIZE)
    res_ref[:, 2] = dv_ref[...].astype(jnp.bfloat16).reshape(blocks, step, HEAD_SIZE)


def attend_backward(me, qkv, out, lse, grad_own, grad_other, rows):
    blocks, step = qkv.shape[0], HEAD_SIZE
    length = blocks * step
    lse = lse.reshape(length // rows, 1, rows)
    return pl.pallas_call(
        functools.partial(bwd_kernel, rows=rows),
        out_shape=jax.ShapeDtypeStruct((blocks, 3, step, HEAD_SIZE), jnp.bfloat16),
        in_specs=[pl.BlockSpec(memory_space=pltpu.SMEM)]
        + [pl.BlockSpec(memory_space=pltpu.VMEM)] * 5,
        out_specs=pl.BlockSpec(memory_space=pltpu.VMEM),
        scratch_shapes=[
            pltpu.VMEM((blocks, step, HEAD_SIZE), jnp.bfloat16),
            pltpu.VMEM((rows, HEAD_SIZE), jnp.float32),
            pltpu.VMEM((length, HEAD_SIZE), jnp.float32),
            pltpu.VMEM((length, HEAD_SIZE), jnp.float32),
        ],
        compiler_params=pltpu.CompilerParams(vmem_limit_bytes=VMEM_LIMIT),
        cost_estimate=pl.CostEstimate(
            flops=20 * length * length * HEAD_SIZE,
            bytes_accessed=16 * length * HEAD_SIZE,
            transcendentals=length * length // 2,
        ),
        name="attend_backward",
    )(me, qkv, out, lse, grad_own, grad_other)


def pack_kernel(q_ref, k_ref, v_ref, kind_ref, out_ref):
    step = q_ref.shape[0]
    kind = jnp.broadcast_to(kind_ref[...].astype(jnp.float32), (KIND_ROWS, HEAD_SIZE))
    for h in range(2 * PACK):
        at = slice(h * HEAD_SIZE, (h + 1) * HEAD_SIZE)
        for w, ref in enumerate((q_ref, k_ref, v_ref)):
            out_ref[h // 2, h % 2, 0, w * step : (w + 1) * step] = ref[:, at]
        out_ref[h // 2, h % 2, 0, 3 * step :] = kind.astype(jnp.bfloat16)


def owner(*tail):
    per = 4 // PACK
    return pl.BlockSpec(
        (PACK, 2, 1, *tail), lambda g: (g % per, 0, g // per, *([0] * len(tail)))
    )


def pack_heads(arrays, kind):
    step, width = arrays[0].shape
    flat = pl.BlockSpec((step, 2 * PACK * HEAD_SIZE), lambda g: (0, g))
    tall = 3 * step + KIND_ROWS
    return pl.pallas_call(
        pack_kernel,
        grid=(16 // PACK,),
        out_shape=jax.ShapeDtypeStruct((4, 2, 4, tall, HEAD_SIZE), jnp.bfloat16),
        in_specs=[flat] * 3 + [pl.BlockSpec((1, step), lambda g: (0, 0))],
        out_specs=owner(tall, HEAD_SIZE),
        name="pack_heads",
    )(*arrays, kind)


def unpack_kernel(in_ref, q_ref, k_ref, v_ref):
    for h in range(2 * PACK):
        at = slice(h * HEAD_SIZE, (h + 1) * HEAD_SIZE)
        for w, ref in enumerate((q_ref, k_ref, v_ref)):
            ref[:, at] = in_ref[h // 2, h % 2, 0, w]


def unpack_heads(stacked):
    step = stacked.shape[-2]
    flat = pl.BlockSpec((step, 2 * PACK * HEAD_SIZE), lambda g: (0, g))
    return pl.pallas_call(
        unpack_kernel,
        grid=(16 // PACK,),
        out_shape=[jax.ShapeDtypeStruct((step, 32 * HEAD_SIZE), jnp.bfloat16)] * 3,
        in_specs=[owner(3, step, HEAD_SIZE)],
        out_specs=[flat] * 3,
        name="unpack_heads",
    )(stacked)


def kind_spec(step):
    return pl.BlockSpec((1, 2, 4, KIND_ROWS, HEAD_SIZE), lambda g: (g, 0, 0, 3 * step // KIND_ROWS, 0))


def is_image(kind_ref, me, b):
    row = kind_ref[0, me, b].astype(jnp.float32)[0:1]
    return jnp.broadcast_to(row, (row.shape[1], row.shape[1])).T > 0.5


def pair_rows(w_ref, kind, me):
    return [w_ref[:, y, kind].reshape(HEAD_SIZE, w_ref.shape[-1]) for y in (me, 1 - me)]


def project_back_kernel(me_ref, up_ref, kind_ref, w_ref, own_ref, other_ref):
    count, step, width = up_ref.shape
    me = me_ref[0]
    upstream = up_ref[...].reshape(count * step, width)
    text = mm(upstream, jnp.concatenate(pair_rows(w_ref, 0, me), axis=0), NT)
    image = mm(upstream, jnp.concatenate(pair_rows(w_ref, 1, me), axis=0), NT)
    for b in range(count):
        mask = is_image(kind_ref, me, b)
        rows = slice(b * step, (b + 1) * step)
        for y, ref in enumerate((own_ref, other_ref)):
            at = slice(y * HEAD_SIZE, (y + 1) * HEAD_SIZE)
            ref[b] = jnp.where(mask, image[rows, at], text[rows, at]).astype(jnp.bfloat16)


def project_back(me, upstream, kinds, weights, group=4):
    count, step, width = upstream.shape
    half = pl.BlockSpec((group, step, HEAD_SIZE), lambda g: (g, 0, 0))
    return pl.pallas_call(
        project_back_kernel,
        grid=(count // group,),
        out_shape=[jax.ShapeDtypeStruct((count, step, HEAD_SIZE), jnp.bfloat16)] * 2,
        in_specs=[
            pl.BlockSpec(memory_space=pltpu.SMEM),
            pl.BlockSpec((group, step, width), lambda g: (g, 0, 0)),
            kind_spec(step),
            pl.BlockSpec(memory_space=pltpu.VMEM),
        ],
        out_specs=[half] * 2,
        compiler_params=pltpu.CompilerParams(vmem_limit_bytes=VMEM_LIMIT),
        cost_estimate=pl.CostEstimate(
            flops=2 * count * step * weights.size, bytes_accessed=2 * upstream.size, transcendentals=0
        ),
        name="project_back",
    )(me, upstream, kinds, weights)


def project_kernel(me_ref, own_ref, other_ref, kind_ref, w_ref, out_ref):
    count, step, _ = own_ref.shape
    me = me_ref[0]
    rows = []
    for b in range(count):
        mask = is_image(kind_ref, me, b)
        parts = [ref[b].astype(jnp.float32) for ref in (own_ref, other_ref)]
        masked = [jnp.where(mask, 0.0, p) for p in parts] + [jnp.where(mask, p, 0.0) for p in parts]
        rows.append(jnp.concatenate(masked, axis=1))
    left = jnp.concatenate(rows, axis=0).astype(jnp.bfloat16)
    right = jnp.concatenate(pair_rows(w_ref, 0, me) + pair_rows(w_ref, 1, me), axis=0)
    out_ref[...] = mm(left, right).astype(out_ref.dtype)


def project(me, own, other, kinds, weights, group=4):
    count, step, _ = own.shape
    width = weights.shape[-1]
    half = pl.BlockSpec((group, step, HEAD_SIZE), lambda g: (g, 0, 0))
    return pl.pallas_call(
        project_kernel,
        grid=(count // group,),
        out_shape=jax.ShapeDtypeStruct((count * step, width), jnp.bfloat16),
        in_specs=[
            pl.BlockSpec(memory_space=pltpu.SMEM),
            half,
            half,
            kind_spec(step),
            pl.BlockSpec(memory_space=pltpu.VMEM),
        ],
        out_specs=pl.BlockSpec((group * step, width), lambda g: (g, 0)),
        compiler_params=pltpu.CompilerParams(vmem_limit_bytes=VMEM_LIMIT),
        cost_estimate=pl.CostEstimate(
            flops=2 * count * step * weights.size,
            bytes_accessed=2 * count * step * width,
            transcendentals=0,
        ),
        name="project",
    )(me, own, other, kinds, weights)


CTX = ("z", "yh", "x")


def exchange(blocks, axis):
    return lax.all_to_all(blocks, axis, split_axis=0, concat_axis=0, tiled=True)


def per_device(query_proj, key_proj, value_proj, modality, out_weight, grad_projected):
    step = query_proj.shape[1]
    me = lax.axis_index("yh").astype(jnp.int32).reshape(1)
    partner = [(0, 1), (1, 0)]
    swap = [(f * 4 + x, x * 4 + f) for f in range(4) for x in range(4)]

    upstream = lax.all_gather(grad_projected[0], ("z", "x"), axis=0)
    shard = lax.ppermute(out_weight, ("fsdp", "x"), swap)

    packed = pack_heads((query_proj[0], key_proj[0], value_proj[0]), modality)
    qkv = exchange(packed.reshape(32, *packed.shape[3:]), CTX)
    kinds = qkv.reshape(packed.shape)
    shard, qkv = lax.optimization_barrier((shard, qkv))
    weights = exchange(jnp.broadcast_to(shard, (8, *shard.shape)), ("fsdp", "yh"))
    weights = weights.reshape(4, 2, *shard.shape)

    attention, own, other, lse = attend_forward(me, qkv, FWD_ROWS)
    other = lax.ppermute(other, "yh", partner)
    partial = project(me, own, other, kinds, weights)
    projected = lax.psum_scatter(partial, ("z", "x"), scatter_dimension=0, tiled=True)
    upstream, partial = lax.optimization_barrier((upstream, partial))
    grad_own, grad_other = project_back(me, upstream, kinds, weights)
    grad_other = lax.ppermute(grad_other, "yh", partner)

    grads = attend_backward(me, qkv, attention, lse, grad_own, grad_other, BWD_ROWS)
    grads = exchange(grads, CTX).reshape(4, 2, 4, *grads.shape[1:])
    grad_query, grad_key, grad_value = unpack_heads(grads)
    return projected[None], grad_query[None], grad_key[None], grad_value[None]


def solution(mesh):
    grid = jax.sharding.Mesh(mesh.devices.reshape(-1, 4, 2, 4), ("fsdp", *CTX))
    rows = P("fsdp", CTX, None)
    placed = (rows, rows, rows, P("fsdp", CTX), P(None, ("fsdp", *CTX), None), rows)
    return jax.shard_map(
        per_device,
        mesh=grid,
        in_specs=placed,
        out_specs=(rows,) * 4,
        check_vma=False,
    )
```

```python
import functools, math
import jax, jax.numpy as jnp
from jax import lax
from jax.experimental import pallas as pl
from jax.experimental.pallas import tpu as pltpu
from jax.sharding import PartitionSpec as P

HEAD_SIZE = 128
LOG2E = math.log2(math.e)
NT = (((1,), (1,)), ((), ()))
TN = (((0,), (0,)), ((), ()))
VMEM_LIMIT = 56 * 1024 * 1024
FWD_ROWS = 1024
BWD_ROWS = 1024
KIND_ROWS = 16
PACK = 4


def mm(a, b, dims=(((1,), (0,)), ((), ()))):
    return lax.dot_general(a, b, dims, preferred_element_type=jnp.float32)


def visible(shape, key_dim, shift):
    keys = lax.broadcasted_iota(jnp.int32, shape, key_dim)
    return keys + shift <= lax.broadcasted_iota(jnp.int32, shape, 1 - key_dim)


def fwd_kernel(
    me_ref, qkv_ref, out_ref, own_ref, other_ref, lse_ref, even_ref, odd_ref, total_ref, acc_ref, *, rows
):
    blocks = qkv_ref.shape[0]
    step = HEAD_SIZE
    per = rows // step
    count = blocks // per
    half = rows // 2
    factor = HEAD_SIZE**-0.5 * LOG2E
    stores = (even_ref, odd_ref)

    def get(which, first, size):
        part = qkv_ref[pl.ds(first, size // step), which * step : (which + 1) * step]
        return part.reshape(size, HEAD_SIZE)

    def fold(op, start, s):
        for c in range(0, s.shape[1], HEAD_SIZE):
            start = op(start, s[:, c : c + HEAD_SIZE])
        return start

    def scores(i, j, top):
        s = mm(get(0, i * per, rows), get(1, j * per, rows), NT) * factor
        stores[i % 2][j] = s
        return fold(jnp.maximum, top, s)

    def values(i, j, high):
        p = jnp.exp2(stores[i % 2][j] - high)
        total_ref[...] = fold(jnp.add, total_ref[...], p)
        acc_ref[...] += mm(p.astype(jnp.bfloat16), get(2, j * per, rows))

    def last_scores(i, top):
        highs = []
        for part in range(2):
            size = half * (part + 1)
            at = slice(part * half, (part + 1) * half)
            s = mm(get(0, i * per + part * per // 2, half), get(1, i * per, size), NT) * factor
            s = jnp.where(visible(s.shape, 1, -part * half), s, -jnp.inf)
            stores[i % 2][i, at, :size] = s
            highs.append(jnp.max(fold(jnp.maximum, top[at], s), axis=1, keepdims=True))
        return highs

    def last_values(i, highs):
        for part in range(2):
            size = half * (part + 1)
            at = slice(part * half, (part + 1) * half)
            p = jnp.exp2(stores[i % 2][i, at, :size] - highs[part])
            total = jnp.sum(fold(jnp.add, total_ref[at], p), axis=1, keepdims=True)
            acc = acc_ref[at] + mm(p.astype(jnp.bfloat16), get(2, i * per, size))
            out = (acc / total).astype(jnp.bfloat16)
            first = i * per + part * per // 2
            out_ref[first : first + per // 2] = out.reshape(-1, step, HEAD_SIZE)
            lse = jnp.broadcast_to(highs[part] + jnp.log2(total), (half, HEAD_SIZE))
            lse_ref[i, :, at] = lse.T[0:1]

    low = jnp.full((rows, HEAD_SIZE), -jnp.inf, jnp.float32)
    highs = last_scores(0, low)
    for i in range(count):
        total_ref[...] = jnp.zeros_like(total_ref)
        acc_ref[...] = jnp.zeros_like(acc_ref)
        high = jnp.concatenate(highs, axis=0)
        top = low

        def both(j, top):
            values(i, j, high)
            return scores(i + 1, j, top) if i + 1 < count else top

        top = lax.fori_loop(0, i, both, top)
        if i + 1 < count:
            top = scores(i + 1, i, top)
        last_values(i, highs)
        if i + 1 < count:
            highs = last_scores(i + 1, top)
    me = me_ref[0]
    half = blocks // 8
    for z in range(4):
        own_ref[z * half : (z + 1) * half] = out_ref[pl.ds((2 * z + me) * half, half)]
        other_ref[z * half : (z + 1) * half] = out_ref[pl.ds((2 * z + 1 - me) * half, half)]


def attend_forward(me, qkv, rows):
    blocks, step = qkv.shape[0], HEAD_SIZE
    length = blocks * step
    return pl.pallas_call(
        functools.partial(fwd_kernel, rows=rows),
        out_shape=(
            jax.ShapeDtypeStruct((blocks, step, HEAD_SIZE), jnp.bfloat16),
            jax.ShapeDtypeStruct((blocks // 2, step, HEAD_SIZE), jnp.bfloat16),
            jax.ShapeDtypeStruct((blocks // 2, step, HEAD_SIZE), jnp.bfloat16),
            jax.ShapeDtypeStruct((length // rows, 1, rows), jnp.float32),
        ),
        in_specs=[
            pl.BlockSpec(memory_space=pltpu.SMEM),
            pl.BlockSpec(memory_space=pltpu.VMEM),
        ],
        out_specs=[pl.BlockSpec(memory_space=pltpu.VMEM)] * 4,
        scratch_shapes=[
            pltpu.VMEM((length // rows - 1, rows, rows), jnp.float32),
            pltpu.VMEM((length // rows, rows, rows), jnp.float32),
        ]
        + [pltpu.VMEM((rows, HEAD_SIZE), jnp.float32)] * 2,
        compiler_params=pltpu.CompilerParams(vmem_limit_bytes=VMEM_LIMIT),
        cost_estimate=pl.CostEstimate(
            flops=12 * length * length * HEAD_SIZE,
            bytes_accessed=8 * length * HEAD_SIZE,
            transcendentals=length * length // 2,
        ),
        name="attend_forward",
    )(me, qkv)


def bwd_kernel(
    me_ref, qkv_ref, out_ref, lse_ref, own_ref, other_ref, res_ref, grad_ref, dq_ref, dk_ref, dv_ref, *, rows
):
    blocks = qkv_ref.shape[0]
    step = HEAD_SIZE
    per = rows // step
    count = blocks // per
    scale = HEAD_SIZE**-0.5
    factor = scale * LOG2E

    def get(which, first, size):
        part = qkv_ref[pl.ds(first, size // step), which * step : (which + 1) * step]
        return part.reshape(size, HEAD_SIZE)

    me = me_ref[0]
    half = blocks // 8
    for z in range(4):
        grad_ref[pl.ds((2 * z + me) * half, half)] = own_ref[z * half : (z + 1) * half]
        grad_ref[pl.ds((2 * z + 1 - me) * half, half)] = other_ref[z * half : (z + 1) * half]
    dk_ref[...] = jnp.zeros_like(dk_ref)
    dv_ref[...] = jnp.zeros_like(dv_ref)

    def query_block(i, _):
        query = get(0, i * per, rows)
        grad = grad_ref[pl.ds(i * per, per)].reshape(rows, HEAD_SIZE)
        attn = out_ref[pl.ds(i * per, per)].reshape(rows, HEAD_SIZE)
        prod = grad.astype(jnp.float32) * attn.astype(jnp.float32)
        delta = jnp.sum(prod.T, axis=0, keepdims=True)
        lse = lse_ref[i]
        dq_ref[...] = jnp.zeros_like(dq_ref)

        def key_block(j, size, at, shift=None):
            key = get(1, j * per, size)
            to = pl.ds(j * rows, size)
            p = jnp.exp2(mm(key, query[at], NT) * factor - lse[:, at])
            if shift is not None:
                p = jnp.where(visible(p.shape, 0, shift), p, 0.0)
            dv_ref[to] += mm(p.astype(jnp.bfloat16), grad[at])
            ds = p * (mm(get(2, j * per, size), grad[at], NT) - delta[:, at]) * scale
            ds = ds.astype(jnp.bfloat16)
            dk_ref[to] += mm(ds, query[at])
            dq_ref[at] += mm(ds, key, TN)

        def body(j, _):
            key_block(j, rows, slice(0, rows))
            return 0

        lax.fori_loop(0, i, body, 0)
        middle = rows // 2
        key_block(i, middle, slice(0, middle), 0)
        key_block(i, rows, slice(middle, rows), -middle)
        done = dq_ref[...].astype(jnp.bfloat16).reshape(per, step, HEAD_SIZE)
        res_ref[pl.ds(i * per, per), 0] = done
        return 0

    lax.fori_loop(0, count, query_block, 0)
    res_ref[:, 1] = dk_ref[...].astype(jnp.bfloat16).reshape(blocks, step, HEAD_SIZE)
    res_ref[:, 2] = dv_ref[...].astype(jnp.bfloat16).reshape(blocks, step, HEAD_SIZE)


def attend_backward(me, qkv, out, lse, grad_own, grad_other, rows):
    blocks, step = qkv.shape[0], HEAD_SIZE
    length = blocks * step
    lse = lse.reshape(length // rows, 1, rows)
    return pl.pallas_call(
        functools.partial(bwd_kernel, rows=rows),
        out_shape=jax.ShapeDtypeStruct((blocks, 3, step, HEAD_SIZE), jnp.bfloat16),
        in_specs=[pl.BlockSpec(memory_space=pltpu.SMEM)]
        + [pl.BlockSpec(memory_space=pltpu.VMEM)] * 5,
        out_specs=pl.BlockSpec(memory_space=pltpu.VMEM),
        scratch_shapes=[
            pltpu.VMEM((blocks, step, HEAD_SIZE), jnp.bfloat16),
            pltpu.VMEM((rows, HEAD_SIZE), jnp.float32),
            pltpu.VMEM((length, HEAD_SIZE), jnp.float32),
            pltpu.VMEM((length, HEAD_SIZE), jnp.float32),
        ],
        compiler_params=pltpu.CompilerParams(vmem_limit_bytes=VMEM_LIMIT),
        cost_estimate=pl.CostEstimate(
            flops=20 * length * length * HEAD_SIZE,
            bytes_accessed=16 * length * HEAD_SIZE,
            transcendentals=length * length // 2,
        ),
        name="attend_backward",
    )(me, qkv, out, lse, grad_own, grad_other)


def pack_kernel(q_ref, k_ref, v_ref, kind_ref, out_ref):
    step = q_ref.shape[0]
    kind = jnp.broadcast_to(kind_ref[...].astype(jnp.float32), (KIND_ROWS, HEAD_SIZE))
    for h in range(2 * PACK):
        at = slice(h * HEAD_SIZE, (h + 1) * HEAD_SIZE)
        for w, ref in enumerate((q_ref, k_ref, v_ref)):
            out_ref[h // 2, h % 2, 0, w * step : (w + 1) * step] = ref[:, at]
        out_ref[h // 2, h % 2, 0, 3 * step :] = kind.astype(jnp.bfloat16)


def owner(*tail):
    per = 4 // PACK
    return pl.BlockSpec(
        (PACK, 2, 1, *tail), lambda g: (g % per, 0, g // per, *([0] * len(tail)))
    )


def pack_heads(arrays, kind):
    step, width = arrays[0].shape
    flat = pl.BlockSpec((step, 2 * PACK * HEAD_SIZE), lambda g: (0, g))
    tall = 3 * step + KIND_ROWS
    return pl.pallas_call(
        pack_kernel,
        grid=(16 // PACK,),
        out_shape=jax.ShapeDtypeStruct((4, 2, 4, tall, HEAD_SIZE), jnp.bfloat16),
        in_specs=[flat] * 3 + [pl.BlockSpec((1, step), lambda g: (0, 0))],
        out_specs=owner(tall, HEAD_SIZE),
        name="pack_heads",
    )(*arrays, kind)


def unpack_kernel(in_ref, q_ref, k_ref, v_ref):
    for h in range(2 * PACK):
        at = slice(h * HEAD_SIZE, (h + 1) * HEAD_SIZE)
        for w, ref in enumerate((q_ref, k_ref, v_ref)):
            ref[:, at] = in_ref[h // 2, h % 2, 0, w]


def unpack_heads(stacked):
    step = stacked.shape[-2]
    flat = pl.BlockSpec((step, 2 * PACK * HEAD_SIZE), lambda g: (0, g))
    return pl.pallas_call(
        unpack_kernel,
        grid=(16 // PACK,),
        out_shape=[jax.ShapeDtypeStruct((step, 32 * HEAD_SIZE), jnp.bfloat16)] * 3,
        in_specs=[owner(3, step, HEAD_SIZE)],
        out_specs=[flat] * 3,
        name="unpack_heads",
    )(stacked)


def kind_spec(step):
    return pl.BlockSpec((1, 2, 4, KIND_ROWS, HEAD_SIZE), lambda g: (g, 0, 0, 3 * step // KIND_ROWS, 0))


def is_image(kind_ref, me, b):
    row = kind_ref[0, me, b].astype(jnp.float32)[0:1]
    return jnp.broadcast_to(row, (row.shape[1], row.shape[1])).T > 0.5


def pair_rows(w_ref, kind, me):
    return [w_ref[:, y, kind].reshape(HEAD_SIZE, w_ref.shape[-1]) for y in (me, 1 - me)]


def project_back_kernel(me_ref, up_ref, kind_ref, w_ref, own_ref, other_ref):
    count, step, width = up_ref.shape
    me = me_ref[0]
    upstream = up_ref[...].reshape(count * step, width)
    text = mm(upstream, jnp.concatenate(pair_rows(w_ref, 0, me), axis=0), NT)
    image = mm(upstream, jnp.concatenate(pair_rows(w_ref, 1, me), axis=0), NT)
    for b in range(count):
        mask = is_image(kind_ref, me, b)
        rows = slice(b * step, (b + 1) * step)
        for y, ref in enumerate((own_ref, other_ref)):
            at = slice(y * HEAD_SIZE, (y + 1) * HEAD_SIZE)
            ref[b] = jnp.where(mask, image[rows, at], text[rows, at]).astype(jnp.bfloat16)


def project_back(me, upstream, kinds, weights, group=4):
    count, step, width = upstream.shape
    half = pl.BlockSpec((group, step, HEAD_SIZE), lambda g: (g, 0, 0))
    return pl.pallas_call(
        project_back_kernel,
        grid=(count // group,),
        out_shape=[jax.ShapeDtypeStruct((count, step, HEAD_SIZE), jnp.bfloat16)] * 2,
        in_specs=[
            pl.BlockSpec(memory_space=pltpu.SMEM),
            pl.BlockSpec((group, step, width), lambda g: (g, 0, 0)),
            kind_spec(step),
            pl.BlockSpec(memory_space=pltpu.VMEM),
        ],
        out_specs=[half] * 2,
        compiler_params=pltpu.CompilerParams(vmem_limit_bytes=VMEM_LIMIT),
        cost_estimate=pl.CostEstimate(
            flops=2 * count * step * weights.size, bytes_accessed=2 * upstream.size, transcendentals=0
        ),
        name="project_back",
    )(me, upstream, kinds, weights)


def project_kernel(me_ref, own_ref, other_ref, kind_ref, w_ref, out_ref):
    count, step, _ = own_ref.shape
    me = me_ref[0]
    rows = []
    for b in range(count):
        mask = is_image(kind_ref, me, b)
        parts = [ref[b].astype(jnp.float32) for ref in (own_ref, other_ref)]
        masked = [jnp.where(mask, 0.0, p) for p in parts] + [jnp.where(mask, p, 0.0) for p in parts]
        rows.append(jnp.concatenate(masked, axis=1))
    left = jnp.concatenate(rows, axis=0).astype(jnp.bfloat16)
    right = jnp.concatenate(pair_rows(w_ref, 0, me) + pair_rows(w_ref, 1, me), axis=0)
    out_ref[...] = mm(left, right).astype(out_ref.dtype)


def project(me, own, other, kinds, weights, group=4):
    count, step, _ = own.shape
    width = weights.shape[-1]
    half = pl.BlockSpec((group, step, HEAD_SIZE), lambda g: (g, 0, 0))
    return pl.pallas_call(
        project_kernel,
        grid=(count // group,),
        out_shape=jax.ShapeDtypeStruct((count * step, width), jnp.bfloat16),
        in_specs=[
            pl.BlockSpec(memory_space=pltpu.SMEM),
            half,
            half,
            kind_spec(step),
            pl.BlockSpec(memory_space=pltpu.VMEM),
        ],
        out_specs=pl.BlockSpec((group * step, width), lambda g: (g, 0)),
        compiler_params=pltpu.CompilerParams(vmem_limit_bytes=VMEM_LIMIT),
        cost_estimate=pl.CostEstimate(
            flops=2 * count * step * weights.size,
            bytes_accessed=2 * count * step * width,
            transcendentals=0,
        ),
        name="project",
    )(me, own, other, kinds, weights)


CTX = ("z", "yh", "x")


def exchange(blocks, axis):
    return lax.all_to_all(blocks, axis, split_axis=0, concat_axis=0, tiled=True)


def per_device(query_proj, key_proj, value_proj, modality, out_weight, grad_projected):
    step = query_proj.shape[1]
    me = lax.axis_index("yh").astype(jnp.int32).reshape(1)
    partner = [(0, 1), (1, 0)]
    swap = [(f * 4 + x, x * 4 + f) for f in range(4) for x in range(4)]

    packed = pack_heads((query_proj[0], key_proj[0], value_proj[0]), modality)
    upstream = lax.all_gather(grad_projected[0], ("z", "x"), axis=0)
    shard = lax.ppermute(out_weight, ("fsdp", "x"), swap)
    qkv = exchange(packed.reshape(32, *packed.shape[3:]), CTX)
    kinds = qkv.reshape(packed.shape)
    shard, qkv = lax.optimization_barrier((shard, qkv))
    weights = exchange(jnp.broadcast_to(shard, (8, *shard.shape)), ("fsdp", "yh"))
    weights = weights.reshape(4, 2, *shard.shape)

    attention, own, other, lse = attend_forward(me, qkv, FWD_ROWS)
    other = lax.ppermute(other, "yh", partner)
    partial = project(me, own, other, kinds, weights)
    projected = lax.psum_scatter(partial, ("z", "x"), scatter_dimension=0, tiled=True)
    upstream, partial = lax.optimization_barrier((upstream, partial))
    grad_own, grad_other = project_back(me, upstream, kinds, weights)
    grad_other = lax.ppermute(grad_other, "yh", partner)

    grads = attend_backward(me, qkv, attention, lse, grad_own, grad_other, BWD_ROWS)
    grads = exchange(grads, CTX).reshape(4, 2, 4, *grads.shape[1:])
    grad_query, grad_key, grad_value = unpack_heads(grads)
    return projected[None], grad_query[None], grad_key[None], grad_value[None]


def solution(mesh):
    grid = jax.sharding.Mesh(mesh.devices.reshape(-1, 4, 2, 4), ("fsdp", *CTX))
    rows = P("fsdp", CTX, None)
    placed = (rows, rows, rows, P("fsdp", CTX), P(None, ("fsdp", *CTX), None), rows)
    return jax.shard_map(
        per_device,
        mesh=grid,
        in_specs=placed,
        out_specs=(rows,) * 4,
        check_vma=False,
    )
```

```python
import functools, math
import jax, jax.numpy as jnp
from jax import lax
from jax.experimental import pallas as pl
from jax.experimental.pallas import tpu as pltpu
from jax.sharding import PartitionSpec as P

HEAD_SIZE = 128
LOG2E = math.log2(math.e)
NT = (((1,), (1,)), ((), ()))
TN = (((0,), (0,)), ((), ()))
VMEM_LIMIT = 56 * 1024 * 1024
FWD_ROWS = 1024
BWD_ROWS = 1024
KIND_ROWS = 16
PACK = 4


def mm(a, b, dims=(((1,), (0,)), ((), ()))):
    return lax.dot_general(a, b, dims, preferred_element_type=jnp.float32)


def visible(shape, key_dim, shift):
    keys = lax.broadcasted_iota(jnp.int32, shape, key_dim)
    return keys + shift <= lax.broadcasted_iota(jnp.int32, shape, 1 - key_dim)


def fwd_kernel(
    me_ref, qkv_ref, out_ref, own_ref, other_ref, lse_ref, even_ref, odd_ref, total_ref, acc_ref, *, rows
):
    blocks = qkv_ref.shape[0]
    step = HEAD_SIZE
    per = rows // step
    count = blocks // per
    half = rows // 2
    factor = HEAD_SIZE**-0.5 * LOG2E
    stores = (even_ref, odd_ref)

    def get(which, first, size):
        part = qkv_ref[pl.ds(first, size // step), which * step : (which + 1) * step]
        return part.reshape(size, HEAD_SIZE)

    def fold(op, start, s):
        for c in range(0, s.shape[1], HEAD_SIZE):
            start = op(start, s[:, c : c + HEAD_SIZE])
        return start

    def scores(i, j, top):
        s = mm(get(0, i * per, rows), get(1, j * per, rows), NT) * factor
        stores[i % 2][j] = s
        return fold(jnp.maximum, top, s)

    def values(i, j, high):
        p = jnp.exp2(stores[i % 2][j] - high)
        total_ref[...] = fold(jnp.add, total_ref[...], p)
        acc_ref[...] += mm(p.astype(jnp.bfloat16), get(2, j * per, rows))

    def last_scores(i, top):
        highs = []
        for part in range(2):
            size = half * (part + 1)
            at = slice(part * half, (part + 1) * half)
            s = mm(get(0, i * per + part * per // 2, half), get(1, i * per, size), NT) * factor
            s = jnp.where(visible(s.shape, 1, -part * half), s, -jnp.inf)
            stores[i % 2][i, at, :size] = s
            highs.append(jnp.max(fold(jnp.maximum, top[at], s), axis=1, keepdims=True))
        return highs

    def last_values(i, highs):
        for part in range(2):
            size = half * (part + 1)
            at = slice(part * half, (part + 1) * half)
            p = jnp.exp2(stores[i % 2][i, at, :size] - highs[part])
            total = jnp.sum(fold(jnp.add, total_ref[at], p), axis=1, keepdims=True)
            acc = acc_ref[at] + mm(p.astype(jnp.bfloat16), get(2, i * per, size))
            out = (acc / total).astype(jnp.bfloat16)
            first = i * per + part * per // 2
            out_ref[first : first + per // 2] = out.reshape(-1, step, HEAD_SIZE)
            lse = jnp.broadcast_to(highs[part] + jnp.log2(total), (half, HEAD_SIZE))
            lse_ref[i, :, at] = lse.T[0:1]

    low = jnp.full((rows, HEAD_SIZE), -jnp.inf, jnp.float32)
    highs = last_scores(0, low)
    for i in range(count):
        total_ref[...] = jnp.zeros_like(total_ref)
        acc_ref[...] = jnp.zeros_like(acc_ref)
        high = jnp.concatenate(highs, axis=0)
        top = low

        def both(j, top):
            values(i, j, high)
            return scores(i + 1, j, top) if i + 1 < count else top

        top = lax.fori_loop(0, i, both, top)
        if i + 1 < count:
            top = scores(i + 1, i, top)
        last_values(i, highs)
        if i + 1 < count:
            highs = last_scores(i + 1, top)
    me = me_ref[0]
    half = blocks // 8
    for z in range(4):
        own_ref[z * half : (z + 1) * half] = out_ref[pl.ds((2 * z + me) * half, half)]
        other_ref[z * half : (z + 1) * half] = out_ref[pl.ds((2 * z + 1 - me) * half, half)]


def attend_forward(me, qkv, rows):
    blocks, step = qkv.shape[0], HEAD_SIZE
    length = blocks * step
    return pl.pallas_call(
        functools.partial(fwd_kernel, rows=rows),
        out_shape=(
            jax.ShapeDtypeStruct((blocks, step, HEAD_SIZE), jnp.bfloat16),
            jax.ShapeDtypeStruct((blocks // 2, step, HEAD_SIZE), jnp.bfloat16),
            jax.ShapeDtypeStruct((blocks // 2, step, HEAD_SIZE), jnp.bfloat16),
            jax.ShapeDtypeStruct((length // rows, 1, rows), jnp.float32),
        ),
        in_specs=[
            pl.BlockSpec(memory_space=pltpu.SMEM),
            pl.BlockSpec(memory_space=pltpu.VMEM),
        ],
        out_specs=[pl.BlockSpec(memory_space=pltpu.VMEM)] * 4,
        scratch_shapes=[
            pltpu.VMEM((length // rows - 1, rows, rows), jnp.float32),
            pltpu.VMEM((length // rows, rows, rows), jnp.float32),
        ]
        + [pltpu.VMEM((rows, HEAD_SIZE), jnp.float32)] * 2,
        compiler_params=pltpu.CompilerParams(vmem_limit_bytes=VMEM_LIMIT),
        cost_estimate=pl.CostEstimate(
            flops=12 * length * length * HEAD_SIZE,
            bytes_accessed=8 * length * HEAD_SIZE,
            transcendentals=length * length // 2,
        ),
        name="attend_forward",
    )(me, qkv)


def bwd_kernel(
    me_ref, qkv_ref, out_ref, lse_ref, own_ref, other_ref, res_ref, grad_ref, dq_ref, dk_ref, dv_ref, *, rows
):
    blocks = qkv_ref.shape[0]
    step = HEAD_SIZE
    per = rows // step
    count = blocks // per
    scale = HEAD_SIZE**-0.5
    factor = scale * LOG2E

    def get(which, first, size):
        part = qkv_ref[pl.ds(first, size // step), which * step : (which + 1) * step]
        return part.reshape(size, HEAD_SIZE)

    me = me_ref[0]
    half = blocks // 8
    for z in range(4):
        grad_ref[pl.ds((2 * z + me) * half, half)] = own_ref[z * half : (z + 1) * half]
        grad_ref[pl.ds((2 * z + 1 - me) * half, half)] = other_ref[z * half : (z + 1) * half]
    dk_ref[...] = jnp.zeros_like(dk_ref)
    dv_ref[...] = jnp.zeros_like(dv_ref)

    def query_block(i, _):
        query = get(0, i * per, rows)
        grad = grad_ref[pl.ds(i * per, per)].reshape(rows, HEAD_SIZE)
        attn = out_ref[pl.ds(i * per, per)].reshape(rows, HEAD_SIZE)
        prod = grad.astype(jnp.float32) * attn.astype(jnp.float32)
        delta = jnp.sum(prod.T, axis=0, keepdims=True)
        lse = lse_ref[i]
        dq_ref[...] = jnp.zeros_like(dq_ref)

        def key_block(j, size, at, shift=None):
            key = get(1, j * per, size)
            to = pl.ds(j * rows, size)
            p = jnp.exp2(mm(key, query[at], NT) * factor - lse[:, at])
            if shift is not None:
                p = jnp.where(visible(p.shape, 0, shift), p, 0.0)
            dv_ref[to] += mm(p.astype(jnp.bfloat16), grad[at])
            ds = p * (mm(get(2, j * per, size), grad[at], NT) - delta[:, at]) * scale
            ds = ds.astype(jnp.bfloat16)
            dk_ref[to] += mm(ds, query[at])
            dq_ref[at] += mm(ds, key, TN)

        def body(j, _):
            key_block(j, rows, slice(0, rows))
            return 0

        lax.fori_loop(0, i, body, 0)
        middle = rows // 2
        key_block(i, middle, slice(0, middle), 0)
        key_block(i, rows, slice(middle, rows), -middle)
        done = dq_ref[...].astype(jnp.bfloat16).reshape(per, step, HEAD_SIZE)
        res_ref[pl.ds(i * per, per), 0] = done
        return 0

    lax.fori_loop(0, count, query_block, 0)
    res_ref[:, 1] = dk_ref[...].astype(jnp.bfloat16).reshape(blocks, step, HEAD_SIZE)
    res_ref[:, 2] = dv_ref[...].astype(jnp.bfloat16).reshape(blocks, step, HEAD_SIZE)


def attend_backward(me, qkv, out, lse, grad_own, grad_other, rows):
    blocks, step = qkv.shape[0], HEAD_SIZE
    length = blocks * step
    lse = lse.reshape(length // rows, 1, rows)
    return pl.pallas_call(
        functools.partial(bwd_kernel, rows=rows),
        out_shape=jax.ShapeDtypeStruct((blocks, 3, step, HEAD_SIZE), jnp.bfloat16),
        in_specs=[pl.BlockSpec(memory_space=pltpu.SMEM)]
        + [pl.BlockSpec(memory_space=pltpu.VMEM)] * 5,
        out_specs=pl.BlockSpec(memory_space=pltpu.VMEM),
        scratch_shapes=[
            pltpu.VMEM((blocks, step, HEAD_SIZE), jnp.bfloat16),
            pltpu.VMEM((rows, HEAD_SIZE), jnp.float32),
            pltpu.VMEM((length, HEAD_SIZE), jnp.float32),
            pltpu.VMEM((length, HEAD_SIZE), jnp.float32),
        ],
        compiler_params=pltpu.CompilerParams(vmem_limit_bytes=VMEM_LIMIT),
        cost_estimate=pl.CostEstimate(
            flops=20 * length * length * HEAD_SIZE,
            bytes_accessed=16 * length * HEAD_SIZE,
            transcendentals=length * length // 2,
        ),
        name="attend_backward",
    )(me, qkv, out, lse, grad_own, grad_other)


def pack_kernel(q_ref, k_ref, v_ref, kind_ref, out_ref):
    step = q_ref.shape[0]
    kind = jnp.broadcast_to(kind_ref[...].astype(jnp.float32), (KIND_ROWS, HEAD_SIZE))
    for h in range(2 * PACK):
        at = slice(h * HEAD_SIZE, (h + 1) * HEAD_SIZE)
        for w, ref in enumerate((q_ref, k_ref, v_ref)):
            out_ref[h // 2, h % 2, 0, w * step : (w + 1) * step] = ref[:, at]
        out_ref[h // 2, h % 2, 0, 3 * step :] = kind.astype(jnp.bfloat16)


def owner(*tail):
    per = 4 // PACK
    return pl.BlockSpec(
        (PACK, 2, 1, *tail), lambda g: (g % per, 0, g // per, *([0] * len(tail)))
    )


def pack_heads(arrays, kind):
    step, width = arrays[0].shape
    flat = pl.BlockSpec((step, 2 * PACK * HEAD_SIZE), lambda g: (0, g))
    tall = 3 * step + KIND_ROWS
    return pl.pallas_call(
        pack_kernel,
        grid=(16 // PACK,),
        out_shape=jax.ShapeDtypeStruct((4, 2, 4, tall, HEAD_SIZE), jnp.bfloat16),
        in_specs=[flat] * 3 + [pl.BlockSpec((1, step), lambda g: (0, 0))],
        out_specs=owner(tall, HEAD_SIZE),
        name="pack_heads",
    )(*arrays, kind)


def unpack_kernel(in_ref, q_ref, k_ref, v_ref):
    for h in range(2 * PACK):
        at = slice(h * HEAD_SIZE, (h + 1) * HEAD_SIZE)
        for w, ref in enumerate((q_ref, k_ref, v_ref)):
            ref[:, at] = in_ref[h // 2, h % 2, 0, w]


def unpack_heads(stacked):
    step = stacked.shape[-2]
    flat = pl.BlockSpec((step, 2 * PACK * HEAD_SIZE), lambda g: (0, g))
    return pl.pallas_call(
        unpack_kernel,
        grid=(16 // PACK,),
        out_shape=[jax.ShapeDtypeStruct((step, 32 * HEAD_SIZE), jnp.bfloat16)] * 3,
        in_specs=[owner(3, step, HEAD_SIZE)],
        out_specs=[flat] * 3,
        name="unpack_heads",
    )(stacked)


def kind_spec(step):
    return pl.BlockSpec((1, 2, 4, KIND_ROWS, HEAD_SIZE), lambda g: (g, 0, 0, 3 * step // KIND_ROWS, 0))


def is_image(kind_ref, me, b):
    row = kind_ref[0, me, b].astype(jnp.float32)[0:1]
    return jnp.broadcast_to(row, (row.shape[1], row.shape[1])).T > 0.5


def head_rows(w_ref, kind, turn):
    rows = [w_ref[jnp.bitwise_xor(turn, x), kind] for x in range(4)]
    return jnp.concatenate(rows, axis=0)


def project_back_kernel(me_ref, up_ref, kind_ref, mine_ref, theirs_ref, own_ref, other_ref):
    count, step, width = up_ref.shape
    me = me_ref[0]
    upstream = up_ref[...].reshape(count * step, width)
    text, image = [
        mm(
            upstream,
            jnp.concatenate([head_rows(w, k, me_ref[1]) for w in (mine_ref, theirs_ref)], axis=0),
            NT,
        )
        for k in range(2)
    ]
    for b in range(count):
        mask = is_image(kind_ref, me, b)
        rows = slice(b * step, (b + 1) * step)
        for y, ref in enumerate((own_ref, other_ref)):
            at = slice(y * HEAD_SIZE, (y + 1) * HEAD_SIZE)
            ref[b] = jnp.where(mask, image[rows, at], text[rows, at]).astype(jnp.bfloat16)


def project_back(me, upstream, kinds, weights, group=4):
    count, step, width = upstream.shape
    half = pl.BlockSpec((group, step, HEAD_SIZE), lambda g: (g, 0, 0))
    return pl.pallas_call(
        project_back_kernel,
        grid=(count // group,),
        out_shape=[jax.ShapeDtypeStruct((count, step, HEAD_SIZE), jnp.bfloat16)] * 2,
        in_specs=[
            pl.BlockSpec(memory_space=pltpu.SMEM),
            pl.BlockSpec((group, step, width), lambda g: (g, 0, 0)),
            kind_spec(step),
            pl.BlockSpec(memory_space=pltpu.VMEM),
            pl.BlockSpec(memory_space=pltpu.VMEM),
        ],
        out_specs=[half] * 2,
        compiler_params=pltpu.CompilerParams(vmem_limit_bytes=VMEM_LIMIT),
        cost_estimate=pl.CostEstimate(
            flops=4 * count * step * weights[0].size, bytes_accessed=2 * upstream.size, transcendentals=0
        ),
        name="project_back",
    )(me, upstream, kinds, *weights)


def project_kernel(me_ref, own_ref, other_ref, kind_ref, mine_ref, theirs_ref, out_ref):
    count, step, _ = own_ref.shape
    me = me_ref[0]
    rows = []
    for b in range(count):
        mask = is_image(kind_ref, me, b)
        parts = [ref[b].astype(jnp.float32) for ref in (own_ref, other_ref)]
        masked = [jnp.where(mask, 0.0, p) for p in parts] + [jnp.where(mask, p, 0.0) for p in parts]
        rows.append(jnp.concatenate(masked, axis=1))
    left = jnp.concatenate(rows, axis=0).astype(jnp.bfloat16)
    right = [head_rows(w, k, me_ref[1]) for k in range(2) for w in (mine_ref, theirs_ref)]
    right = jnp.concatenate(right, axis=0)
    out_ref[...] = mm(left, right).astype(out_ref.dtype)


def project(me, own, other, kinds, weights, group=4):
    count, step, _ = own.shape
    width = weights[0].shape[-1]
    half = pl.BlockSpec((group, step, HEAD_SIZE), lambda g: (g, 0, 0))
    return pl.pallas_call(
        project_kernel,
        grid=(count // group,),
        out_shape=jax.ShapeDtypeStruct((count * step, width), jnp.bfloat16),
        in_specs=[
            pl.BlockSpec(memory_space=pltpu.SMEM),
            half,
            half,
            kind_spec(step),
            pl.BlockSpec(memory_space=pltpu.VMEM),
            pl.BlockSpec(memory_space=pltpu.VMEM),
        ],
        out_specs=pl.BlockSpec((group * step, width), lambda g: (g, 0)),
        compiler_params=pltpu.CompilerParams(vmem_limit_bytes=VMEM_LIMIT),
        cost_estimate=pl.CostEstimate(
            flops=4 * count * step * weights[0].size,
            bytes_accessed=2 * count * step * width,
            transcendentals=0,
        ),
        name="project",
    )(me, own, other, kinds, *weights)


CTX = ("z", "yh", "x")


def exchange(blocks, axis):
    return lax.all_to_all(blocks, axis, split_axis=0, concat_axis=0, tiled=True)


def per_device(query_proj, key_proj, value_proj, modality, out_weight, grad_projected):
    step = query_proj.shape[1]
    me = jnp.stack([lax.axis_index("yh"), lax.axis_index("fsdp")]).astype(jnp.int32)
    partner = [(0, 1), (1, 0)]
    swap = [(f * 4 + x, x * 4 + f) for f in range(4) for x in range(4)]

    upstream = lax.all_gather(grad_projected[0], ("z", "x"), axis=0)
    mine = lax.ppermute(out_weight, ("fsdp", "x"), swap)[None]
    for bit in (1, 2):
        sent = lax.ppermute(mine, "fsdp", [(f, f ^ bit) for f in range(4)])
        mine = jnp.concatenate([mine, sent], axis=0)
    weights = mine, lax.ppermute(mine, "yh", partner)

    packed = pack_heads((query_proj[0], key_proj[0], value_proj[0]), modality)
    qkv = exchange(packed.reshape(32, *packed.shape[3:]), CTX)
    kinds = qkv.reshape(packed.shape)

    attention, own, other, lse = attend_forward(me, qkv, FWD_ROWS)
    other = lax.ppermute(other, "yh", partner)
    partial = project(me, own, other, kinds, weights)
    projected = lax.psum_scatter(partial, ("z", "x"), scatter_dimension=0, tiled=True)
    upstream, partial = lax.optimization_barrier((upstream, partial))
    grad_own, grad_other = project_back(me, upstream, kinds, weights)
    grad_other = lax.ppermute(grad_other, "yh", partner)

    grads = attend_backward(me, qkv, attention, lse, grad_own, grad_other, BWD_ROWS)
    grads = exchange(grads, CTX).reshape(4, 2, 4, *grads.shape[1:])
    grad_query, grad_key, grad_value = unpack_heads(grads)
    return projected[None], grad_query[None], grad_key[None], grad_value[None]


def solution(mesh):
    grid = jax.sharding.Mesh(mesh.devices.reshape(-1, 4, 2, 4), ("fsdp", *CTX))
    rows = P("fsdp", CTX, None)
    placed = (rows, rows, rows, P("fsdp", CTX), P(None, ("fsdp", *CTX), None), rows)
    return jax.shard_map(
        per_device,
        mesh=grid,
        in_specs=placed,
        out_specs=(rows,) * 4,
        check_vma=False,
    )
```

```python
import functools, math
import jax, jax.numpy as jnp
from jax import lax
from jax.experimental import pallas as pl
from jax.experimental.pallas import tpu as pltpu
from jax.sharding import PartitionSpec as P

HEAD_SIZE = 128
LOG2E = math.log2(math.e)
NT = (((1,), (1,)), ((), ()))
TN = (((0,), (0,)), ((), ()))
VMEM_LIMIT = 56 * 1024 * 1024
FWD_ROWS = 1024
BWD_ROWS = 1024
KIND_ROWS = 16
PACK = 4


def mm(a, b, dims=(((1,), (0,)), ((), ()))):
    return lax.dot_general(a, b, dims, preferred_element_type=jnp.float32)


def visible(shape, key_dim, shift):
    keys = lax.broadcasted_iota(jnp.int32, shape, key_dim)
    return keys + shift <= lax.broadcasted_iota(jnp.int32, shape, 1 - key_dim)


def fwd_kernel(
    me_ref, qkv_ref, out_ref, own_ref, other_ref, lse_ref, even_ref, odd_ref, total_ref, acc_ref, *, rows
):
    blocks = qkv_ref.shape[0]
    step = HEAD_SIZE
    per = rows // step
    count = blocks // per
    half = rows // 2
    factor = HEAD_SIZE**-0.5 * LOG2E
    stores = (even_ref, odd_ref)

    def get(which, first, size):
        part = qkv_ref[pl.ds(first, size // step), which * step : (which + 1) * step]
        return part.reshape(size, HEAD_SIZE)

    def fold(op, start, s):
        for c in range(0, s.shape[1], HEAD_SIZE):
            start = op(start, s[:, c : c + HEAD_SIZE])
        return start

    def scores(i, j, top):
        s = mm(get(0, i * per, rows), get(1, j * per, rows), NT) * factor
        stores[i % 2][j] = s
        return fold(jnp.maximum, top, s)

    def values(i, j, high):
        p = jnp.exp2(stores[i % 2][j] - high)
        total_ref[...] = fold(jnp.add, total_ref[...], p)
        acc_ref[...] += mm(p.astype(jnp.bfloat16), get(2, j * per, rows))

    def last_scores(i, top):
        highs = []
        for part in range(2):
            size = half * (part + 1)
            at = slice(part * half, (part + 1) * half)
            s = mm(get(0, i * per + part * per // 2, half), get(1, i * per, size), NT) * factor
            s = jnp.where(visible(s.shape, 1, -part * half), s, -jnp.inf)
            stores[i % 2][i, at, :size] = s
            highs.append(jnp.max(fold(jnp.maximum, top[at], s), axis=1, keepdims=True))
        return highs

    def last_values(i, highs):
        for part in range(2):
            size = half * (part + 1)
            at = slice(part * half, (part + 1) * half)
            p = jnp.exp2(stores[i % 2][i, at, :size] - highs[part])
            total = jnp.sum(fold(jnp.add, total_ref[at], p), axis=1, keepdims=True)
            acc = acc_ref[at] + mm(p.astype(jnp.bfloat16), get(2, i * per, size))
            out = (acc / total).astype(jnp.bfloat16)
            first = i * per + part * per // 2
            out_ref[first : first + per // 2] = out.reshape(-1, step, HEAD_SIZE)
            lse = jnp.broadcast_to(highs[part] + jnp.log2(total), (half, HEAD_SIZE))
            lse_ref[i, :, at] = lse.T[0:1]

    low = jnp.full((rows, HEAD_SIZE), -jnp.inf, jnp.float32)
    highs = last_scores(0, low)
    for i in range(count):
        total_ref[...] = jnp.zeros_like(total_ref)
        acc_ref[...] = jnp.zeros_like(acc_ref)
        high = jnp.concatenate(highs, axis=0)
        top = low

        def both(j, top):
            values(i, j, high)
            return scores(i + 1, j, top) if i + 1 < count else top

        top = lax.fori_loop(0, i, both, top)
        if i + 1 < count:
            top = scores(i + 1, i, top)
        last_values(i, highs)
        if i + 1 < count:
            highs = last_scores(i + 1, top)
    me = me_ref[0]
    half = blocks // 8
    for z in range(4):
        own_ref[z * half : (z + 1) * half] = out_ref[pl.ds((2 * z + me) * half, half)]
        other_ref[z * half : (z + 1) * half] = out_ref[pl.ds((2 * z + 1 - me) * half, half)]


def attend_forward(me, qkv, rows):
    blocks, step = qkv.shape[0], HEAD_SIZE
    length = blocks * step
    return pl.pallas_call(
        functools.partial(fwd_kernel, rows=rows),
        out_shape=(
            jax.ShapeDtypeStruct((blocks, step, HEAD_SIZE), jnp.bfloat16),
            jax.ShapeDtypeStruct((blocks // 2, step, HEAD_SIZE), jnp.bfloat16),
            jax.ShapeDtypeStruct((blocks // 2, step, HEAD_SIZE), jnp.bfloat16),
            jax.ShapeDtypeStruct((length // rows, 1, rows), jnp.float32),
        ),
        in_specs=[
            pl.BlockSpec(memory_space=pltpu.SMEM),
            pl.BlockSpec(memory_space=pltpu.VMEM),
        ],
        out_specs=[pl.BlockSpec(memory_space=pltpu.VMEM)] * 4,
        scratch_shapes=[
            pltpu.VMEM((length // rows - 1, rows, rows), jnp.float32),
            pltpu.VMEM((length // rows, rows, rows), jnp.float32),
        ]
        + [pltpu.VMEM((rows, HEAD_SIZE), jnp.float32)] * 2,
        compiler_params=pltpu.CompilerParams(vmem_limit_bytes=VMEM_LIMIT),
        cost_estimate=pl.CostEstimate(
            flops=12 * length * length * HEAD_SIZE,
            bytes_accessed=8 * length * HEAD_SIZE,
            transcendentals=length * length // 2,
        ),
        name="attend_forward",
    )(me, qkv)


def bwd_half(y, qkv_ref, out_ref, lse_ref, grad_ref, dq_ref, dk_ref, dv_ref, write, *, rows):
    blocks = qkv_ref.shape[0]
    step = HEAD_SIZE
    per = rows // step
    half = per // 2
    width = rows // 2
    scale = HEAD_SIZE**-0.5
    factor = scale * LOG2E

    def get(which, first, size):
        part = qkv_ref[pl.ds(first, size // step), which * step : (which + 1) * step]
        return part.reshape(size, HEAD_SIZE)

    def query_block(z, _):
        first = z * per + y * half
        query = get(0, first, width)
        grad = grad_ref[pl.ds(z * half, half)].reshape(width, HEAD_SIZE)
        attn = out_ref[pl.ds(first, half)].reshape(width, HEAD_SIZE)
        prod = grad.astype(jnp.float32) * attn.astype(jnp.float32)
        delta = jnp.sum(prod.T, axis=0, keepdims=True)
        lse = lse_ref[2 * z + y]
        dq_ref[...] = jnp.zeros_like(dq_ref)

        def key_block(j, size, shift=None):
            key = get(1, j * per, size)
            to = pl.ds(j * rows, size)
            p = jnp.exp2(mm(key, query, NT) * factor - lse)
            if shift is not None:
                p = jnp.where(visible(p.shape, 0, shift), p, 0.0)
            dv_ref[to] += mm(p.astype(jnp.bfloat16), grad)
            ds = (p * (mm(get(2, j * per, size), grad, NT) - delta) * scale).astype(jnp.bfloat16)
            dk_ref[to] += mm(ds, query)
            dq_ref[...] += mm(ds, key, TN)

        def body(j, _):
            key_block(j, rows)
            return 0

        lax.fori_loop(0, z, body, 0)

        @pl.when(y == 0)
        def _():
            key_block(z, width, 0)

        @pl.when(y == 1)
        def _():
            key_block(z, rows, -width)

        write(z, first, dq_ref[...].astype(jnp.bfloat16).reshape(half, step, HEAD_SIZE))
        return 0

    lax.fori_loop(0, blocks // per, query_block, 0)


def bwd_first_kernel(
    me_ref, qkv_ref, out_ref, lse_ref, grad_ref, done_ref, dk_ref, dv_ref, dq_ref, *, rows
):
    dk_ref[...] = jnp.zeros_like(dk_ref)
    dv_ref[...] = jnp.zeros_like(dv_ref)
    half = rows // HEAD_SIZE // 2

    def write(z, first, value):
        done_ref[pl.ds(z * half, half)] = value

    bwd_half(me_ref[0], qkv_ref, out_ref, lse_ref, grad_ref, dq_ref, dk_ref, dv_ref, write, rows=rows)


def bwd_second_kernel(
    me_ref, qkv_ref, out_ref, lse_ref, grad_ref, done_ref, dk_ref, dv_ref, res_ref, dq_ref, *, rows
):
    blocks = qkv_ref.shape[0]
    per = rows // HEAD_SIZE
    half = per // 2
    me = me_ref[0]
    for z in range(blocks // per):
        res_ref[pl.ds(z * per + me * half, half), 0] = done_ref[z * half : (z + 1) * half]

    def write(z, first, value):
        res_ref[pl.ds(first, half), 0] = value

    bwd_half(1 - me, qkv_ref, out_ref, lse_ref, grad_ref, dq_ref, dk_ref, dv_ref, write, rows=rows)
    res_ref[:, 1] = dk_ref[...].astype(jnp.bfloat16).reshape(blocks, HEAD_SIZE, HEAD_SIZE)
    res_ref[:, 2] = dv_ref[...].astype(jnp.bfloat16).reshape(blocks, HEAD_SIZE, HEAD_SIZE)


def attend_backward(me, qkv, out, lse, grad_own, grad_other, rows):
    blocks, step = qkv.shape[0], HEAD_SIZE
    length = blocks * step
    lse = lse.reshape(2 * length // rows, 1, rows // 2)
    vmem = pl.BlockSpec(memory_space=pltpu.VMEM)
    common = dict(
        scratch_shapes=[pltpu.VMEM((rows // 2, HEAD_SIZE), jnp.float32)],
        compiler_params=pltpu.CompilerParams(vmem_limit_bytes=VMEM_LIMIT),
        cost_estimate=pl.CostEstimate(
            flops=10 * length * length * HEAD_SIZE,
            bytes_accessed=16 * length * HEAD_SIZE,
            transcendentals=length * length // 4,
        ),
    )
    sums = jax.ShapeDtypeStruct((length, HEAD_SIZE), jnp.float32)
    done, dk, dv = pl.pallas_call(
        functools.partial(bwd_first_kernel, rows=rows),
        out_shape=[jax.ShapeDtypeStruct((blocks // 2, step, HEAD_SIZE), jnp.bfloat16), sums, sums],
        in_specs=[pl.BlockSpec(memory_space=pltpu.SMEM)] + [vmem] * 4,
        out_specs=[vmem] * 3,
        name="backward_own",
        **common,
    )(me, qkv, out, lse, grad_own)
    return pl.pallas_call(
        functools.partial(bwd_second_kernel, rows=rows),
        out_shape=jax.ShapeDtypeStruct((blocks, 3, step, HEAD_SIZE), jnp.bfloat16),
        in_specs=[pl.BlockSpec(memory_space=pltpu.SMEM)] + [vmem] * 7,
        out_specs=vmem,
        name="backward_other",
        **common,
    )(me, qkv, out, lse, grad_other, done, dk, dv)


def pack_kernel(q_ref, k_ref, v_ref, kind_ref, out_ref):
    step = q_ref.shape[0]
    kind = jnp.broadcast_to(kind_ref[...].astype(jnp.float32), (KIND_ROWS, HEAD_SIZE))
    for h in range(2 * PACK):
        at = slice(h * HEAD_SIZE, (h + 1) * HEAD_SIZE)
        for w, ref in enumerate((q_ref, k_ref, v_ref)):
            out_ref[h // 2, h % 2, 0, w * step : (w + 1) * step] = ref[:, at]
        out_ref[h // 2, h % 2, 0, 3 * step :] = kind.astype(jnp.bfloat16)


def owner(*tail):
    per = 4 // PACK
    return pl.BlockSpec(
        (PACK, 2, 1, *tail), lambda g: (g % per, 0, g // per, *([0] * len(tail)))
    )


def pack_heads(arrays, kind):
    step, width = arrays[0].shape
    flat = pl.BlockSpec((step, 2 * PACK * HEAD_SIZE), lambda g: (0, g))
    tall = 3 * step + KIND_ROWS
    return pl.pallas_call(
        pack_kernel,
        grid=(16 // PACK,),
        out_shape=jax.ShapeDtypeStruct((4, 2, 4, tall, HEAD_SIZE), jnp.bfloat16),
        in_specs=[flat] * 3 + [pl.BlockSpec((1, step), lambda g: (0, 0))],
        out_specs=owner(tall, HEAD_SIZE),
        name="pack_heads",
    )(*arrays, kind)


def unpack_kernel(in_ref, q_ref, k_ref, v_ref):
    for h in range(2 * PACK):
        at = slice(h * HEAD_SIZE, (h + 1) * HEAD_SIZE)
        for w, ref in enumerate((q_ref, k_ref, v_ref)):
            ref[:, at] = in_ref[h // 2, h % 2, 0, w]


def unpack_heads(stacked):
    step = stacked.shape[-2]
    flat = pl.BlockSpec((step, 2 * PACK * HEAD_SIZE), lambda g: (0, g))
    return pl.pallas_call(
        unpack_kernel,
        grid=(16 // PACK,),
        out_shape=[jax.ShapeDtypeStruct((step, 32 * HEAD_SIZE), jnp.bfloat16)] * 3,
        in_specs=[owner(3, step, HEAD_SIZE)],
        out_specs=[flat] * 3,
        name="unpack_heads",
    )(stacked)


def kind_spec(step):
    return pl.BlockSpec((1, 2, 4, KIND_ROWS, HEAD_SIZE), lambda g: (g, 0, 0, 3 * step // KIND_ROWS, 0))


def is_image(kind_ref, me, b):
    row = kind_ref[0, me, b].astype(jnp.float32)[0:1]
    return jnp.broadcast_to(row, (row.shape[1], row.shape[1])).T > 0.5


def assemble(pair_ref, same_ref, cross_ref, core):
    for low in range(2):
        for ref, side in ((same_ref, core), (cross_ref, 1 - core)):
            for y in range(2):
                pair_ref[:, y, 2 * low + side] = ref[low, y]


def pair_rows(pair_ref, kind, me):
    width = pair_ref.shape[-1]
    return [pair_ref[kind, y].reshape(HEAD_SIZE, width) for y in (me, 1 - me)]


def pair_scratch(weights):
    _, _, kinds, rows, width = weights[0].shape
    return pltpu.VMEM((kinds, 2, 4, rows, width), jnp.bfloat16)


def project_back_kernel(
    me_ref, up_ref, kind_ref, same_ref, cross_ref, own_ref, other_ref, pair_ref
):
    count, step, width = up_ref.shape
    me = me_ref[0]
    upstream = up_ref[...].reshape(count * step, width)

    @pl.when(pl.program_id(0) == 0)
    def _():
        assemble(pair_ref, same_ref, cross_ref, me_ref[1])

    text = mm(upstream, jnp.concatenate(pair_rows(pair_ref, 0, me), axis=0), NT)
    image = mm(upstream, jnp.concatenate(pair_rows(pair_ref, 1, me), axis=0), NT)
    for b in range(count):
        mask = is_image(kind_ref, me, b)
        rows = slice(b * step, (b + 1) * step)
        for y, ref in enumerate((own_ref, other_ref)):
            at = slice(y * HEAD_SIZE, (y + 1) * HEAD_SIZE)
            ref[b] = jnp.where(mask, image[rows, at], text[rows, at]).astype(jnp.bfloat16)


def project_back(me, upstream, kinds, weights, group=4):
    count, step, width = upstream.shape
    half = pl.BlockSpec((group, step, HEAD_SIZE), lambda g: (g, 0, 0))
    return pl.pallas_call(
        project_back_kernel,
        grid=(count // group,),
        out_shape=[jax.ShapeDtypeStruct((count, step, HEAD_SIZE), jnp.bfloat16)] * 2,
        in_specs=[
            pl.BlockSpec(memory_space=pltpu.SMEM),
            pl.BlockSpec((group, step, width), lambda g: (g, 0, 0)),
            kind_spec(step),
            pl.BlockSpec(memory_space=pltpu.VMEM),
            pl.BlockSpec(memory_space=pltpu.VMEM),
        ],
        out_specs=[half] * 2,
        scratch_shapes=[pair_scratch(weights)],
        compiler_params=pltpu.CompilerParams(vmem_limit_bytes=VMEM_LIMIT),
        cost_estimate=pl.CostEstimate(
            flops=4 * count * step * weights[0].size, bytes_accessed=2 * upstream.size, transcendentals=0
        ),
        name="project_back",
    )(me, upstream, kinds, *weights)


def project_kernel(
    me_ref, own_ref, other_ref, kind_ref, same_ref, cross_ref, out_ref, pair_ref
):
    count, step, _ = own_ref.shape
    me = me_ref[0]
    rows = []
    for b in range(count):
        mask = is_image(kind_ref, me, b)
        parts = [ref[b].astype(jnp.float32) for ref in (own_ref, other_ref)]
        masked = [jnp.where(mask, 0.0, p) for p in parts] + [jnp.where(mask, p, 0.0) for p in parts]
        rows.append(jnp.concatenate(masked, axis=1))
    left = jnp.concatenate(rows, axis=0).astype(jnp.bfloat16)

    @pl.when(pl.program_id(0) == 0)
    def _():
        assemble(pair_ref, same_ref, cross_ref, me_ref[1])

    right = jnp.concatenate(pair_rows(pair_ref, 0, me) + pair_rows(pair_ref, 1, me), axis=0)
    out_ref[...] = mm(left, right).astype(out_ref.dtype)


def project(me, own, other, kinds, weights, group=4):
    count, step, _ = own.shape
    width = weights[0].shape[-1]
    half = pl.BlockSpec((group, step, HEAD_SIZE), lambda g: (g, 0, 0))
    return pl.pallas_call(
        project_kernel,
        grid=(count // group,),
        out_shape=jax.ShapeDtypeStruct((count * step, width), jnp.bfloat16),
        in_specs=[
            pl.BlockSpec(memory_space=pltpu.SMEM),
            half,
            half,
            kind_spec(step),
            pl.BlockSpec(memory_space=pltpu.VMEM),
            pl.BlockSpec(memory_space=pltpu.VMEM),
        ],
        out_specs=pl.BlockSpec((group * step, width), lambda g: (g, 0)),
        scratch_shapes=[pair_scratch(weights)],
        compiler_params=pltpu.CompilerParams(vmem_limit_bytes=VMEM_LIMIT),
        cost_estimate=pl.CostEstimate(
            flops=4 * count * step * weights[0].size,
            bytes_accessed=2 * count * step * width,
            transcendentals=0,
        ),
        name="project",
    )(me, own, other, kinds, *weights)


FSDP = ("low", "core")
CTX = ("z", "yh", "x")


def exchange(blocks, axis):
    return lax.all_to_all(blocks, axis, split_axis=0, concat_axis=0, tiled=True)


def per_device(query_proj, key_proj, value_proj, modality, out_weight, grad_projected):
    step = query_proj.shape[1]
    me = jnp.stack([lax.axis_index("yh"), lax.axis_index("core")]).astype(jnp.int32)
    partner = [(0, 1), (1, 0)]
    swap = [(f * 4 + x, x * 4 + f) for f in range(4) for x in range(4)]

    upstream = lax.all_gather(grad_projected[0], ("z", "x"), axis=0)
    shard = lax.ppermute(out_weight, ("low", "core", "x"), swap)
    shard = jnp.broadcast_to(shard, (4, *shard.shape))
    packed = pack_heads((query_proj[0], key_proj[0], value_proj[0]), modality)
    qkv = exchange(packed.reshape(32, *packed.shape[3:]), CTX)
    kinds = qkv.reshape(packed.shape)
    shard, qkv = lax.optimization_barrier((shard, qkv))
    same = exchange(shard, ("low", "yh")).reshape(2, 2, *out_weight.shape)

    attention, own, other, lse = attend_forward(me, qkv, FWD_ROWS)
    same, other = lax.optimization_barrier((same, other))
    weights = same, lax.ppermute(same, "core", partner)
    other = lax.ppermute(other, "yh", partner)
    partial = project(me, own, other, kinds, weights)
    projected = lax.psum_scatter(partial, ("z", "x"), scatter_dimension=0, tiled=True)
    upstream, partial = lax.optimization_barrier((upstream, partial))
    grad_own, grad_other = project_back(me, upstream, kinds, weights)
    grad_other = lax.ppermute(grad_other, "yh", partner)

    grads = attend_backward(me, qkv, attention, lse, grad_own, grad_other, BWD_ROWS)
    grads = exchange(grads, CTX).reshape(4, 2, 4, *grads.shape[1:])
    grad_query, grad_key, grad_value = unpack_heads(grads)
    return projected[None], grad_query[None], grad_key[None], grad_value[None]


def solution(mesh):
    grid = jax.sharding.Mesh(mesh.devices.reshape(2, 2, 4, 2, 4), ("low", "core", *CTX))
    rows = P(FSDP, CTX, None)
    placed = (rows, rows, rows, P(FSDP, CTX), P(None, (*FSDP, *CTX), None), rows)
    return jax.shard_map(
        per_device,
        mesh=grid,
        in_specs=placed,
        out_specs=(rows,) * 4,
        check_vma=False,
    )
```

```python
import functools, math
import jax, jax.numpy as jnp
from jax import lax
from jax.experimental import pallas as pl
from jax.experimental.pallas import tpu as pltpu
from jax.sharding import PartitionSpec as P

HEAD_SIZE = 128
LOG2E = math.log2(math.e)
NT = (((1,), (1,)), ((), ()))
TN = (((0,), (0,)), ((), ()))
VMEM_LIMIT = 56 * 1024 * 1024
FWD_ROWS = 1024
HALF = 512
BWD_VMEM_LIMIT = 40 * 1024 * 1024
KIND_ROWS = 16
PACK = 4


def mm(a, b, dims=(((1,), (0,)), ((), ()))):
    return lax.dot_general(a, b, dims, preferred_element_type=jnp.float32)


def visible(shape, key_dim, shift):
    keys = lax.broadcasted_iota(jnp.int32, shape, key_dim)
    return keys + shift <= lax.broadcasted_iota(jnp.int32, shape, 1 - key_dim)


def fwd_kernel(
    me_ref, qkv_ref, out_ref, own_ref, other_ref, lse_ref, even_ref, odd_ref, total_ref, acc_ref, *, rows
):
    blocks = qkv_ref.shape[0]
    step = HEAD_SIZE
    per = rows // step
    count = blocks // per
    half = rows // 2
    factor = HEAD_SIZE**-0.5 * LOG2E
    stores = (even_ref, odd_ref)

    def get(which, first, size):
        part = qkv_ref[pl.ds(first, size // step), which * step : (which + 1) * step]
        return part.reshape(size, HEAD_SIZE)

    def fold(op, start, s):
        for c in range(0, s.shape[1], HEAD_SIZE):
            start = op(start, s[:, c : c + HEAD_SIZE])
        return start

    def scores(i, j, top):
        s = mm(get(0, i * per, rows), get(1, j * per, rows), NT) * factor
        stores[i % 2][j] = s
        return fold(jnp.maximum, top, s)

    def values(i, j, high):
        p = jnp.exp2(stores[i % 2][j] - high)
        total_ref[...] = fold(jnp.add, total_ref[...], p)
        acc_ref[...] += mm(p.astype(jnp.bfloat16), get(2, j * per, rows))

    def last_scores(i, top):
        highs = []
        for part in range(2):
            size = half * (part + 1)
            at = slice(part * half, (part + 1) * half)
            s = mm(get(0, i * per + part * per // 2, half), get(1, i * per, size), NT) * factor
            s = jnp.where(visible(s.shape, 1, -part * half), s, -jnp.inf)
            stores[i % 2][i, at, :size] = s
            highs.append(jnp.max(fold(jnp.maximum, top[at], s), axis=1, keepdims=True))
        return highs

    def last_values(i, highs):
        for part in range(2):
            size = half * (part + 1)
            at = slice(part * half, (part + 1) * half)
            p = jnp.exp2(stores[i % 2][i, at, :size] - highs[part])
            total = jnp.sum(fold(jnp.add, total_ref[at], p), axis=1, keepdims=True)
            acc = acc_ref[at] + mm(p.astype(jnp.bfloat16), get(2, i * per, size))
            out = (acc / total).astype(jnp.bfloat16)
            first = i * per + part * per // 2
            out_ref[first : first + per // 2] = out.reshape(-1, step, HEAD_SIZE)
            lse = jnp.broadcast_to(highs[part] + jnp.log2(total), (half, HEAD_SIZE))
            lse_ref[i, :, at] = lse.T[0:1]

    low = jnp.full((rows, HEAD_SIZE), -jnp.inf, jnp.float32)
    highs = last_scores(0, low)
    for i in range(count):
        total_ref[...] = jnp.zeros_like(total_ref)
        acc_ref[...] = jnp.zeros_like(acc_ref)
        high = jnp.concatenate(highs, axis=0)
        top = low

        def both(j, top):
            values(i, j, high)
            return scores(i + 1, j, top) if i + 1 < count else top

        top = lax.fori_loop(0, i, both, top)
        if i + 1 < count:
            top = scores(i + 1, i, top)
        last_values(i, highs)
        if i + 1 < count:
            highs = last_scores(i + 1, top)
    me = me_ref[0]
    half = blocks // 8
    for z in range(4):
        own_ref[z * half : (z + 1) * half] = out_ref[pl.ds((2 * z + me) * half, half)]
        other_ref[z * half : (z + 1) * half] = out_ref[pl.ds((2 * z + 1 - me) * half, half)]


def attend_forward(me, qkv, rows):
    blocks, step = qkv.shape[0], HEAD_SIZE
    length = blocks * step
    return pl.pallas_call(
        functools.partial(fwd_kernel, rows=rows),
        out_shape=(
            jax.ShapeDtypeStruct((blocks, step, HEAD_SIZE), jnp.bfloat16),
            jax.ShapeDtypeStruct((blocks // 2, step, HEAD_SIZE), jnp.bfloat16),
            jax.ShapeDtypeStruct((blocks // 2, step, HEAD_SIZE), jnp.bfloat16),
            jax.ShapeDtypeStruct((length // rows, 1, rows), jnp.float32),
        ),
        in_specs=[
            pl.BlockSpec(memory_space=pltpu.SMEM),
            pl.BlockSpec(memory_space=pltpu.VMEM),
        ],
        out_specs=[pl.BlockSpec(memory_space=pltpu.VMEM)] * 4,
        scratch_shapes=[
            pltpu.VMEM((length // rows - 1, rows, rows), jnp.float32),
            pltpu.VMEM((length // rows, rows, rows), jnp.float32),
        ]
        + [pltpu.VMEM((rows, HEAD_SIZE), jnp.float32)] * 2,
        compiler_params=pltpu.CompilerParams(vmem_limit_bytes=VMEM_LIMIT),
        cost_estimate=pl.CostEstimate(
            flops=12 * length * length * HEAD_SIZE,
            bytes_accessed=8 * length * HEAD_SIZE,
            transcendentals=length * length // 2,
        ),
        name="attend_forward",
    )(me, qkv)


def bwd_tools(qkv_ref, out_ref, lse_ref, dq_ref, dk_ref, dv_ref):
    step = HEAD_SIZE
    half = HALF // step
    scale = HEAD_SIZE**-0.5
    factor = scale * LOG2E

    def get(which, first, size):
        part = qkv_ref[pl.ds(first, size // step), which * step : (which + 1) * step]
        return part.reshape(size, HEAD_SIZE)

    def row_delta(grad, attn):
        prod = grad.astype(jnp.float32) * attn.astype(jnp.float32)
        return jnp.sum(prod.T, axis=0, keepdims=True)

    def block(rows, first, size, at, shift=None):
        query, grad, lse, delta = rows
        query, grad, lse, delta = query[at], grad[at], lse[:, at], delta[:, at]
        key = get(1, first, size)
        to = slice(first * step, first * step + size)
        p = jnp.exp2(mm(key, query, NT) * factor - lse)
        if shift is not None:
            p = jnp.where(visible(p.shape, 0, shift), p, 0.0)
        dv_ref[to] += mm(p.astype(jnp.bfloat16), grad)
        ds = (p * (mm(get(2, first, size), grad, NT) - delta) * scale).astype(jnp.bfloat16)
        dk_ref[to] += mm(ds, query)
        dq_ref[at] += mm(ds, key, TN)

    def late_rows(y, grad):
        firsts = [2 * z * half + y * half for z in (2, 3)]
        query = jnp.concatenate([get(0, f, HALF) for f in firsts], axis=0)
        attn = [out_ref[pl.ds(f, half)].reshape(HALF, HEAD_SIZE) for f in firsts]
        lse = jnp.concatenate([lse_ref[2 * z + y] for z in (2, 3)], axis=1)
        rows = query, grad, lse, row_delta(grad, jnp.concatenate(attn, axis=0))
        dq_ref[...] = jnp.zeros_like(dq_ref)
        both, low, high = slice(0, 2 * HALF), slice(0, HALF), slice(HALF, 2 * HALF)
        block(rows, 0, 2 * HALF, both)
        block(rows, 2 * half, 2 * HALF, both)
        block(rows, 4 * half, 2 * HALF, high)

        @pl.when(y == 0)
        def _():
            block(rows, 4 * half, HALF, low, 0)
            block(rows, 6 * half, HALF, high, 0)

        @pl.when(y == 1)
        def _():
            block(rows, 4 * half, 2 * HALF, low, -HALF)
            block(rows, 6 * half, 2 * HALF, high, -HALF)

        return dq_ref[...].astype(jnp.bfloat16).reshape(2 * half, step, HEAD_SIZE)

    def early_rows(z, grad):
        attn = out_ref[2 * z * half : 2 * (z + 1) * half].reshape(2 * HALF, HEAD_SIZE)
        lse = jnp.concatenate([lse_ref[2 * z], lse_ref[2 * z + 1]], axis=1)
        rows = get(0, 2 * z * half, 2 * HALF), grad, lse, row_delta(grad, attn)
        dq_ref[...] = jnp.zeros_like(dq_ref)
        for j in range(z):
            block(rows, 2 * j * half, 2 * HALF, slice(0, 2 * HALF))
        block(rows, 2 * z * half, HALF, slice(0, HALF), 0)
        block(rows, 2 * z * half, 2 * HALF, slice(HALF, 2 * HALF), -HALF)
        return dq_ref[...].astype(jnp.bfloat16).reshape(2 * half, step, HEAD_SIZE)

    return late_rows, early_rows


def bwd_first_kernel(me_ref, qkv_ref, out_ref, lse_ref, grad_ref, done_ref, dk_ref, dv_ref, dq_ref):
    dk_ref[...] = jnp.zeros_like(dk_ref)
    dv_ref[...] = jnp.zeros_like(dv_ref)
    late_rows, _ = bwd_tools(qkv_ref, out_ref, lse_ref, dq_ref, dk_ref, dv_ref)
    late = grad_ref.shape[0] // 2
    done_ref[...] = late_rows(me_ref[0], grad_ref[late:].reshape(2 * HALF, HEAD_SIZE))


def bwd_second_kernel(
    me_ref, qkv_ref, out_ref, lse_ref, own_ref, other_ref, done_ref, dk_ref, dv_ref,
    res_ref, dq_ref, grad_ref
):
    blocks = qkv_ref.shape[0]
    half = HALF // HEAD_SIZE
    late = 2 * half
    me = me_ref[0]
    late_rows, early_rows = bwd_tools(qkv_ref, out_ref, lse_ref, dq_ref, dk_ref, dv_ref)
    for z in range(2):
        grad_ref[pl.ds((2 * z + me) * half, half)] = own_ref[z * half : (z + 1) * half]
        grad_ref[pl.ds((2 * z + 1 - me) * half, half)] = other_ref[z * half : (z + 1) * half]
    other = late_rows(1 - me, other_ref[late:].reshape(2 * HALF, HEAD_SIZE))
    for k in range(2):
        piece = slice(k * half, (k + 1) * half)
        z = k + 2
        res_ref[pl.ds((2 * z + me) * half, half), 0] = done_ref[piece]
        res_ref[pl.ds((2 * z + 1 - me) * half, half), 0] = other[piece]
    for z in range(2):
        at = slice(2 * z * half, 2 * (z + 1) * half)
        res_ref[at, 0] = early_rows(z, grad_ref[at].reshape(2 * HALF, HEAD_SIZE))
    res_ref[:, 1] = dk_ref[...].astype(jnp.bfloat16).reshape(blocks, HEAD_SIZE, HEAD_SIZE)
    res_ref[:, 2] = dv_ref[...].astype(jnp.bfloat16).reshape(blocks, HEAD_SIZE, HEAD_SIZE)


def attend_backward(me, qkv, out, lse, grad_own, grad_other):
    blocks, step = qkv.shape[0], HEAD_SIZE
    length = blocks * step
    lse = lse.reshape(length // HALF, 1, HALF)
    vmem = pl.BlockSpec(memory_space=pltpu.VMEM)
    acc = pltpu.VMEM((2 * HALF, HEAD_SIZE), jnp.float32)
    common = dict(
        compiler_params=pltpu.CompilerParams(vmem_limit_bytes=BWD_VMEM_LIMIT),
        cost_estimate=pl.CostEstimate(
            flops=10 * length * length * HEAD_SIZE,
            bytes_accessed=16 * length * HEAD_SIZE,
            transcendentals=length * length // 4,
        ),
    )
    sums = jax.ShapeDtypeStruct((length, HEAD_SIZE), jnp.float32)
    done, dk, dv = pl.pallas_call(
        bwd_first_kernel,
        out_shape=[jax.ShapeDtypeStruct((blocks // 4, step, HEAD_SIZE), jnp.bfloat16), sums, sums],
        in_specs=[pl.BlockSpec(memory_space=pltpu.SMEM)] + [vmem] * 4,
        out_specs=[vmem] * 3,
        scratch_shapes=[acc],
        name="backward_own",
        **common,
    )(me, qkv, out, lse, grad_own)
    return pl.pallas_call(
        bwd_second_kernel,
        out_shape=jax.ShapeDtypeStruct((blocks, 3, step, HEAD_SIZE), jnp.bfloat16),
        in_specs=[pl.BlockSpec(memory_space=pltpu.SMEM)] + [vmem] * 8,
        out_specs=vmem,
        scratch_shapes=[acc, pltpu.VMEM((blocks // 2, step, HEAD_SIZE), jnp.bfloat16)],
        name="backward_other",
        **common,
    )(me, qkv, out, lse, grad_own, grad_other, done, dk, dv)


def pack_kernel(q_ref, k_ref, v_ref, kind_ref, out_ref):
    step = q_ref.shape[0]
    kind = jnp.broadcast_to(kind_ref[...].astype(jnp.float32), (KIND_ROWS, HEAD_SIZE))
    for h in range(2 * PACK):
        at = slice(h * HEAD_SIZE, (h + 1) * HEAD_SIZE)
        for w, ref in enumerate((q_ref, k_ref, v_ref)):
            out_ref[h // 2, h % 2, 0, w * step : (w + 1) * step] = ref[:, at]
        out_ref[h // 2, h % 2, 0, 3 * step :] = kind.astype(jnp.bfloat16)


def owner(*tail):
    per = 4 // PACK
    return pl.BlockSpec(
        (PACK, 2, 1, *tail), lambda g: (g % per, 0, g // per, *([0] * len(tail)))
    )


def pack_heads(arrays, kind):
    step, width = arrays[0].shape
    flat = pl.BlockSpec((step, 2 * PACK * HEAD_SIZE), lambda g: (0, g))
    tall = 3 * step + KIND_ROWS
    return pl.pallas_call(
        pack_kernel,
        grid=(16 // PACK,),
        out_shape=jax.ShapeDtypeStruct((4, 2, 4, tall, HEAD_SIZE), jnp.bfloat16),
        in_specs=[flat] * 3 + [pl.BlockSpec((1, step), lambda g: (0, 0))],
        out_specs=owner(tall, HEAD_SIZE),
        name="pack_heads",
    )(*arrays, kind)


def unpack_kernel(in_ref, q_ref, k_ref, v_ref):
    for h in range(2 * PACK):
        at = slice(h * HEAD_SIZE, (h + 1) * HEAD_SIZE)
        for w, ref in enumerate((q_ref, k_ref, v_ref)):
            ref[:, at] = in_ref[h // 2, h % 2, 0, w]


def unpack_heads(stacked):
    step = stacked.shape[-2]
    flat = pl.BlockSpec((step, 2 * PACK * HEAD_SIZE), lambda g: (0, g))
    return pl.pallas_call(
        unpack_kernel,
        grid=(16 // PACK,),
        out_shape=[jax.ShapeDtypeStruct((step, 32 * HEAD_SIZE), jnp.bfloat16)] * 3,
        in_specs=[owner(3, step, HEAD_SIZE)],
        out_specs=[flat] * 3,
        name="unpack_heads",
    )(stacked)


def kind_spec(step):
    return pl.BlockSpec((1, 2, 4, KIND_ROWS, HEAD_SIZE), lambda g: (g, 0, 0, 3 * step // KIND_ROWS, 0))


def is_image(kind_ref, me, b):
    row = kind_ref[0, me, b].astype(jnp.float32)[0:1]
    return jnp.broadcast_to(row, (row.shape[1], row.shape[1])).T > 0.5


def assemble(pair_ref, same_ref, cross_ref, core):
    for low in range(2):
        for ref, side in ((same_ref, core), (cross_ref, 1 - core)):
            for y in range(2):
                pair_ref[:, y, 2 * low + side] = ref[low, y]


def pair_rows(pair_ref, kind, me):
    width = pair_ref.shape[-1]
    return [pair_ref[kind, y].reshape(HEAD_SIZE, width) for y in (me, 1 - me)]


def pair_scratch(weights):
    _, _, kinds, rows, width = weights[0].shape
    return pltpu.VMEM((kinds, 2, 4, rows, width), jnp.bfloat16)


def project_back_kernel(
    me_ref, up_ref, kind_ref, same_ref, cross_ref, own_ref, other_ref, pair_ref
):
    count, step, width = up_ref.shape
    me = me_ref[0]
    upstream = up_ref[...].reshape(count * step, width)

    @pl.when(pl.program_id(0) == 0)
    def _():
        assemble(pair_ref, same_ref, cross_ref, me_ref[1])

    text = mm(upstream, jnp.concatenate(pair_rows(pair_ref, 0, me), axis=0), NT)
    image = mm(upstream, jnp.concatenate(pair_rows(pair_ref, 1, me), axis=0), NT)
    for b in range(count):
        mask = is_image(kind_ref, me, b)
        rows = slice(b * step, (b + 1) * step)
        for y, ref in enumerate((own_ref, other_ref)):
            at = slice(y * HEAD_SIZE, (y + 1) * HEAD_SIZE)
            ref[b] = jnp.where(mask, image[rows, at], text[rows, at]).astype(jnp.bfloat16)


def project_back(me, upstream, kinds, weights, group=4):
    count, step, width = upstream.shape
    half = pl.BlockSpec((group, step, HEAD_SIZE), lambda g: (g, 0, 0))
    return pl.pallas_call(
        project_back_kernel,
        grid=(count // group,),
        out_shape=[jax.ShapeDtypeStruct((count, step, HEAD_SIZE), jnp.bfloat16)] * 2,
        in_specs=[
            pl.BlockSpec(memory_space=pltpu.SMEM),
            pl.BlockSpec((group, step, width), lambda g: (g, 0, 0)),
            kind_spec(step),
            pl.BlockSpec(memory_space=pltpu.VMEM),
            pl.BlockSpec(memory_space=pltpu.VMEM),
        ],
        out_specs=[half] * 2,
        scratch_shapes=[pair_scratch(weights)],
        compiler_params=pltpu.CompilerParams(vmem_limit_bytes=VMEM_LIMIT),
        cost_estimate=pl.CostEstimate(
            flops=4 * count * step * weights[0].size, bytes_accessed=2 * upstream.size, transcendentals=0
        ),
        name="project_back",
    )(me, upstream, kinds, *weights)


def project_kernel(
    me_ref, own_ref, other_ref, kind_ref, same_ref, cross_ref, out_ref, pair_ref
):
    count, step, _ = own_ref.shape
    me = me_ref[0]
    rows = []
    for b in range(count):
        mask = is_image(kind_ref, me, b)
        parts = [ref[b].astype(jnp.float32) for ref in (own_ref, other_ref)]
        masked = [jnp.where(mask, 0.0, p) for p in parts] + [jnp.where(mask, p, 0.0) for p in parts]
        rows.append(jnp.concatenate(masked, axis=1))
    left = jnp.concatenate(rows, axis=0).astype(jnp.bfloat16)

    @pl.when(pl.program_id(0) == 0)
    def _():
        assemble(pair_ref, same_ref, cross_ref, me_ref[1])

    right = jnp.concatenate(pair_rows(pair_ref, 0, me) + pair_rows(pair_ref, 1, me), axis=0)
    out_ref[...] = mm(left, right).astype(out_ref.dtype)


def project(me, own, other, kinds, weights, group=4):
    count, step, _ = own.shape
    width = weights[0].shape[-1]
    half = pl.BlockSpec((group, step, HEAD_SIZE), lambda g: (g, 0, 0))
    return pl.pallas_call(
        project_kernel,
        grid=(count // group,),
        out_shape=jax.ShapeDtypeStruct((count * step, width), jnp.bfloat16),
        in_specs=[
            pl.BlockSpec(memory_space=pltpu.SMEM),
            half,
            half,
            kind_spec(step),
            pl.BlockSpec(memory_space=pltpu.VMEM),
            pl.BlockSpec(memory_space=pltpu.VMEM),
        ],
        out_specs=pl.BlockSpec((group * step, width), lambda g: (g, 0)),
        scratch_shapes=[pair_scratch(weights)],
        compiler_params=pltpu.CompilerParams(vmem_limit_bytes=VMEM_LIMIT),
        cost_estimate=pl.CostEstimate(
            flops=4 * count * step * weights[0].size,
            bytes_accessed=2 * count * step * width,
            transcendentals=0,
        ),
        name="project",
    )(me, own, other, kinds, *weights)


FSDP = ("low", "core")
CTX = ("z", "yh", "x")


def exchange(blocks, axis):
    return lax.all_to_all(blocks, axis, split_axis=0, concat_axis=0, tiled=True)


def per_device(query_proj, key_proj, value_proj, modality, out_weight, grad_projected):
    step = query_proj.shape[1]
    me = jnp.stack([lax.axis_index("yh"), lax.axis_index("core")]).astype(jnp.int32)
    partner = [(0, 1), (1, 0)]
    swap = [(f * 4 + x, x * 4 + f) for f in range(4) for x in range(4)]

    upstream = lax.all_gather(grad_projected[0], ("z", "x"), axis=0)
    shard = lax.ppermute(out_weight, ("low", "core", "x"), swap)
    shard = jnp.broadcast_to(shard, (4, *shard.shape))
    packed = pack_heads((query_proj[0], key_proj[0], value_proj[0]), modality)
    qkv = exchange(packed.reshape(32, *packed.shape[3:]), CTX)
    kinds = qkv.reshape(packed.shape)
    shard, qkv = lax.optimization_barrier((shard, qkv))
    same = exchange(shard, ("low", "yh")).reshape(2, 2, *out_weight.shape)

    attention, own, other, lse = attend_forward(me, qkv, FWD_ROWS)
    same, other = lax.optimization_barrier((same, other))
    weights = same, lax.ppermute(same, "core", partner)
    other = lax.ppermute(other, "yh", partner)
    partial = project(me, own, other, kinds, weights)
    projected = lax.psum_scatter(partial, ("z", "x"), scatter_dimension=0, tiled=True)
    upstream, partial = lax.optimization_barrier((upstream, partial))
    grad_own, grad_other = project_back(me, upstream, kinds, weights)
    grad_other = lax.ppermute(grad_other, "yh", partner)

    grads = attend_backward(me, qkv, attention, lse, grad_own, grad_other)
    grads = exchange(grads, CTX).reshape(4, 2, 4, *grads.shape[1:])
    grad_query, grad_key, grad_value = unpack_heads(grads)
    return projected[None], grad_query[None], grad_key[None], grad_value[None]


def solution(mesh):
    grid = jax.sharding.Mesh(mesh.devices.reshape(2, 2, 4, 2, 4), ("low", "core", *CTX))
    rows = P(FSDP, CTX, None)
    placed = (rows, rows, rows, P(FSDP, CTX), P(None, (*FSDP, *CTX), None), rows)
    return jax.shard_map(
        per_device,
        mesh=grid,
        in_specs=placed,
        out_specs=(rows,) * 4,
        check_vma=False,
    )
```

```python
import functools, math
import jax, jax.numpy as jnp
from jax import lax
from jax.experimental import pallas as pl
from jax.experimental.pallas import tpu as pltpu
from jax.sharding import PartitionSpec as P

HEAD_SIZE = 128
LOG2E = math.log2(math.e)
NT = (((1,), (1,)), ((), ()))
TN = (((0,), (0,)), ((), ()))
VMEM_LIMIT = 56 * 1024 * 1024
FWD_ROWS = 1024
HALF = 512
BWD_VMEM_LIMIT = 40 * 1024 * 1024
KIND_ROWS = 16
PACK = 4


def mm(a, b, dims=(((1,), (0,)), ((), ()))):
    return lax.dot_general(a, b, dims, preferred_element_type=jnp.float32)


def visible(shape, key_dim, shift):
    keys = lax.broadcasted_iota(jnp.int32, shape, key_dim)
    return keys + shift <= lax.broadcasted_iota(jnp.int32, shape, 1 - key_dim)


def fwd_kernel(
    qkv_ref, out_ref, sent_ref, lse_ref, even_ref, odd_ref, total_ref, acc_ref, *, rows
):
    blocks = qkv_ref.shape[0]
    step = HEAD_SIZE
    per = rows // step
    count = blocks // per
    half = rows // 2
    factor = HEAD_SIZE**-0.5 * LOG2E
    stores = (even_ref, odd_ref)

    def get(which, first, size):
        part = qkv_ref[pl.ds(first, size // step), which * step : (which + 1) * step]
        return part.reshape(size, HEAD_SIZE)

    def fold(op, start, s):
        for c in range(0, s.shape[1], HEAD_SIZE):
            start = op(start, s[:, c : c + HEAD_SIZE])
        return start

    def scores(i, j, top):
        s = mm(get(0, i * per, rows), get(1, j * per, rows), NT) * factor
        stores[i % 2][j] = s
        return fold(jnp.maximum, top, s)

    def values(i, j, high):
        p = jnp.exp2(stores[i % 2][j] - high)
        total_ref[...] = fold(jnp.add, total_ref[...], p)
        acc_ref[...] += mm(p.astype(jnp.bfloat16), get(2, j * per, rows))

    def last_scores(i, top):
        highs = []
        for part in range(2):
            size = half * (part + 1)
            at = slice(part * half, (part + 1) * half)
            s = mm(get(0, i * per + part * per // 2, half), get(1, i * per, size), NT) * factor
            s = jnp.where(visible(s.shape, 1, -part * half), s, -jnp.inf)
            stores[i % 2][i, at, :size] = s
            highs.append(jnp.max(fold(jnp.maximum, top[at], s), axis=1, keepdims=True))
        return highs

    def last_values(i, highs):
        for part in range(2):
            size = half * (part + 1)
            at = slice(part * half, (part + 1) * half)
            p = jnp.exp2(stores[i % 2][i, at, :size] - highs[part])
            total = jnp.sum(fold(jnp.add, total_ref[at], p), axis=1, keepdims=True)
            acc = acc_ref[at] + mm(p.astype(jnp.bfloat16), get(2, i * per, size))
            out = (acc / total).astype(jnp.bfloat16)
            first = i * per + part * per // 2
            out_ref[first : first + per // 2] = out.reshape(-1, step, HEAD_SIZE)
            lse = jnp.broadcast_to(highs[part] + jnp.log2(total), (half, HEAD_SIZE))
            lse_ref[i, :, at] = lse.T[0:1]

    low = jnp.full((rows, HEAD_SIZE), -jnp.inf, jnp.float32)
    highs = last_scores(0, low)
    for i in range(count):
        total_ref[...] = jnp.zeros_like(total_ref)
        acc_ref[...] = jnp.zeros_like(acc_ref)
        high = jnp.concatenate(highs, axis=0)
        top = low

        def both(j, top):
            values(i, j, high)
            return scores(i + 1, j, top) if i + 1 < count else top

        top = lax.fori_loop(0, i, both, top)
        if i + 1 < count:
            top = scores(i + 1, i, top)
        last_values(i, highs)
        if i + 1 < count:
            highs = last_scores(i + 1, top)
    for z in range(4):
        for group in range(4):
            first = 8 * z + 2 * group
            sent_ref[group, 2 * z : 2 * z + 2] = out_ref[first : first + 2]


def attend_forward(qkv, rows):
    blocks, step = qkv.shape[0], HEAD_SIZE
    length = blocks * step
    return pl.pallas_call(
        functools.partial(fwd_kernel, rows=rows),
        out_shape=(
            jax.ShapeDtypeStruct((blocks, step, HEAD_SIZE), jnp.bfloat16),
            jax.ShapeDtypeStruct((4, blocks // 4, step, HEAD_SIZE), jnp.bfloat16),
            jax.ShapeDtypeStruct((length // rows, 1, rows), jnp.float32),
        ),
        in_specs=[pl.BlockSpec(memory_space=pltpu.VMEM)],
        out_specs=[pl.BlockSpec(memory_space=pltpu.VMEM)] * 3,
        scratch_shapes=[
            pltpu.VMEM((length // rows - 1, rows, rows), jnp.float32),
            pltpu.VMEM((length // rows, rows, rows), jnp.float32),
        ]
        + [pltpu.VMEM((rows, HEAD_SIZE), jnp.float32)] * 2,
        compiler_params=pltpu.CompilerParams(vmem_limit_bytes=VMEM_LIMIT),
        cost_estimate=pl.CostEstimate(
            flops=12 * length * length * HEAD_SIZE,
            bytes_accessed=8 * length * HEAD_SIZE,
            transcendentals=length * length // 2,
        ),
        name="attend_forward",
    )(qkv)


def bwd_tools(qkv_ref, out_ref, lse_ref, dq_ref, dk_ref, dv_ref):
    step = HEAD_SIZE
    half = HALF // step
    scale = HEAD_SIZE**-0.5
    factor = scale * LOG2E

    def get(which, first, size):
        part = qkv_ref[pl.ds(first, size // step), which * step : (which + 1) * step]
        return part.reshape(size, HEAD_SIZE)

    def row_delta(grad, attn):
        prod = grad.astype(jnp.float32) * attn.astype(jnp.float32)
        return jnp.sum(prod.T, axis=0, keepdims=True)

    def block(rows, first, size, at, shift=None):
        query, grad, lse, delta = rows
        query, grad, lse, delta = query[at], grad[at], lse[:, at], delta[:, at]
        key = get(1, first, size)
        to = slice(first * step, first * step + size)
        p = jnp.exp2(mm(key, query, NT) * factor - lse)
        if shift is not None:
            p = jnp.where(visible(p.shape, 0, shift), p, 0.0)
        dv_ref[to] += mm(p.astype(jnp.bfloat16), grad)
        ds = (p * (mm(get(2, first, size), grad, NT) - delta) * scale).astype(jnp.bfloat16)
        dk_ref[to] += mm(ds, query)
        dq_ref[at] += mm(ds, key, TN)

    def late_rows(y, grad):
        firsts = [2 * z * half + y * half for z in (2, 3)]
        query = jnp.concatenate([get(0, f, HALF) for f in firsts], axis=0)
        attn = [out_ref[pl.ds(f, half)].reshape(HALF, HEAD_SIZE) for f in firsts]
        lse = jnp.concatenate([lse_ref[2 * z + y] for z in (2, 3)], axis=1)
        rows = query, grad, lse, row_delta(grad, jnp.concatenate(attn, axis=0))
        dq_ref[...] = jnp.zeros_like(dq_ref)
        both, low, high = slice(0, 2 * HALF), slice(0, HALF), slice(HALF, 2 * HALF)
        block(rows, 0, 2 * HALF, both)
        block(rows, 2 * half, 2 * HALF, both)
        block(rows, 4 * half, 2 * HALF, high)

        @pl.when(y == 0)
        def _():
            block(rows, 4 * half, HALF, low, 0)
            block(rows, 6 * half, HALF, high, 0)

        @pl.when(y == 1)
        def _():
            block(rows, 4 * half, 2 * HALF, low, -HALF)
            block(rows, 6 * half, 2 * HALF, high, -HALF)

        return dq_ref[...].astype(jnp.bfloat16).reshape(2 * half, step, HEAD_SIZE)

    def early_rows(z, grad):
        attn = out_ref[2 * z * half : 2 * (z + 1) * half].reshape(2 * HALF, HEAD_SIZE)
        lse = jnp.concatenate([lse_ref[2 * z], lse_ref[2 * z + 1]], axis=1)
        rows = get(0, 2 * z * half, 2 * HALF), grad, lse, row_delta(grad, attn)
        dq_ref[...] = jnp.zeros_like(dq_ref)
        for j in range(z):
            block(rows, 2 * j * half, 2 * HALF, slice(0, 2 * HALF))
        block(rows, 2 * z * half, HALF, slice(0, HALF), 0)
        block(rows, 2 * z * half, 2 * HALF, slice(HALF, 2 * HALF), -HALF)
        return dq_ref[...].astype(jnp.bfloat16).reshape(2 * half, step, HEAD_SIZE)

    return late_rows, early_rows


def bwd_first_kernel(me_ref, qkv_ref, out_ref, lse_ref, grad_ref, done_ref, dk_ref, dv_ref, dq_ref):
    dk_ref[...] = jnp.zeros_like(dk_ref)
    dv_ref[...] = jnp.zeros_like(dv_ref)
    late_rows, _ = bwd_tools(qkv_ref, out_ref, lse_ref, dq_ref, dk_ref, dv_ref)
    late = grad_ref.shape[0] // 2
    done_ref[...] = late_rows(me_ref[0], grad_ref[late:].reshape(2 * HALF, HEAD_SIZE))


def bwd_second_kernel(
    me_ref, qkv_ref, out_ref, lse_ref, own_ref, other_ref, done_ref, dk_ref, dv_ref,
    res_ref, dq_ref, grad_ref
):
    blocks = qkv_ref.shape[0]
    half = HALF // HEAD_SIZE
    late = 2 * half
    me = me_ref[0]
    late_rows, early_rows = bwd_tools(qkv_ref, out_ref, lse_ref, dq_ref, dk_ref, dv_ref)
    for z in range(2):
        grad_ref[pl.ds((2 * z + me) * half, half)] = own_ref[z * half : (z + 1) * half]
        grad_ref[pl.ds((2 * z + 1 - me) * half, half)] = other_ref[z * half : (z + 1) * half]
    other = late_rows(1 - me, other_ref[late:].reshape(2 * HALF, HEAD_SIZE))
    for k in range(2):
        piece = slice(k * half, (k + 1) * half)
        z = k + 2
        res_ref[pl.ds((2 * z + me) * half, half), 0] = done_ref[piece]
        res_ref[pl.ds((2 * z + 1 - me) * half, half), 0] = other[piece]
    for z in range(2):
        at = slice(2 * z * half, 2 * (z + 1) * half)
        res_ref[at, 0] = early_rows(z, grad_ref[at].reshape(2 * HALF, HEAD_SIZE))
    res_ref[:, 1] = dk_ref[...].astype(jnp.bfloat16).reshape(blocks, HEAD_SIZE, HEAD_SIZE)
    res_ref[:, 2] = dv_ref[...].astype(jnp.bfloat16).reshape(blocks, HEAD_SIZE, HEAD_SIZE)


def attend_backward(me, qkv, out, lse, grad_own, grad_other):
    blocks, step = qkv.shape[0], HEAD_SIZE
    length = blocks * step
    lse = lse.reshape(length // HALF, 1, HALF)
    vmem = pl.BlockSpec(memory_space=pltpu.VMEM)
    acc = pltpu.VMEM((2 * HALF, HEAD_SIZE), jnp.float32)
    common = dict(
        compiler_params=pltpu.CompilerParams(vmem_limit_bytes=BWD_VMEM_LIMIT),
        cost_estimate=pl.CostEstimate(
            flops=10 * length * length * HEAD_SIZE,
            bytes_accessed=16 * length * HEAD_SIZE,
            transcendentals=length * length // 4,
        ),
    )
    sums = jax.ShapeDtypeStruct((length, HEAD_SIZE), jnp.float32)
    done, dk, dv = pl.pallas_call(
        bwd_first_kernel,
        out_shape=[jax.ShapeDtypeStruct((blocks // 4, step, HEAD_SIZE), jnp.bfloat16), sums, sums],
        in_specs=[pl.BlockSpec(memory_space=pltpu.SMEM)] + [vmem] * 4,
        out_specs=[vmem] * 3,
        scratch_shapes=[acc],
        name="backward_own",
        **common,
    )(me, qkv, out, lse, grad_own)
    return pl.pallas_call(
        bwd_second_kernel,
        out_shape=jax.ShapeDtypeStruct((blocks, 3, step, HEAD_SIZE), jnp.bfloat16),
        in_specs=[pl.BlockSpec(memory_space=pltpu.SMEM)] + [vmem] * 8,
        out_specs=vmem,
        scratch_shapes=[acc, pltpu.VMEM((blocks // 2, step, HEAD_SIZE), jnp.bfloat16)],
        name="backward_other",
        **common,
    )(me, qkv, out, lse, grad_own, grad_other, done, dk, dv)


def pack_kernel(q_ref, k_ref, v_ref, kind_ref, out_ref):
    step = q_ref.shape[0]
    kind = jnp.broadcast_to(kind_ref[...].astype(jnp.float32), (KIND_ROWS, HEAD_SIZE))
    for h in range(2 * PACK):
        at = slice(h * HEAD_SIZE, (h + 1) * HEAD_SIZE)
        for w, ref in enumerate((q_ref, k_ref, v_ref)):
            out_ref[h // 2, h % 2, 0, w * step : (w + 1) * step] = ref[:, at]
        out_ref[h // 2, h % 2, 0, 3 * step :] = kind.astype(jnp.bfloat16)


def owner(*tail):
    per = 4 // PACK
    return pl.BlockSpec(
        (PACK, 2, 1, *tail), lambda g: (g % per, 0, g // per, *([0] * len(tail)))
    )


def pack_heads(arrays, kind):
    step, width = arrays[0].shape
    flat = pl.BlockSpec((step, 2 * PACK * HEAD_SIZE), lambda g: (0, g))
    tall = 3 * step + KIND_ROWS
    return pl.pallas_call(
        pack_kernel,
        grid=(16 // PACK,),
        out_shape=jax.ShapeDtypeStruct((4, 2, 4, tall, HEAD_SIZE), jnp.bfloat16),
        in_specs=[flat] * 3 + [pl.BlockSpec((1, step), lambda g: (0, 0))],
        out_specs=owner(tall, HEAD_SIZE),
        name="pack_heads",
    )(*arrays, kind)


def unpack_kernel(in_ref, q_ref, k_ref, v_ref):
    for h in range(2 * PACK):
        at = slice(h * HEAD_SIZE, (h + 1) * HEAD_SIZE)
        for w, ref in enumerate((q_ref, k_ref, v_ref)):
            ref[:, at] = in_ref[h // 2, h % 2, 0, w]


def unpack_heads(stacked):
    step = stacked.shape[-2]
    flat = pl.BlockSpec((step, 2 * PACK * HEAD_SIZE), lambda g: (0, g))
    return pl.pallas_call(
        unpack_kernel,
        grid=(16 // PACK,),
        out_shape=[jax.ShapeDtypeStruct((step, 32 * HEAD_SIZE), jnp.bfloat16)] * 3,
        in_specs=[owner(3, step, HEAD_SIZE)],
        out_specs=[flat] * 3,
        name="unpack_heads",
    )(stacked)


def kind_spec(step):
    return pl.BlockSpec((1, 2, 4, KIND_ROWS, HEAD_SIZE), lambda g: (g, 0, 0, 3 * step // KIND_ROWS, 0))


def is_image(kind_ref, me, b):
    row = kind_ref[0, me, b].astype(jnp.float32)[0:1]
    return jnp.broadcast_to(row, (row.shape[1], row.shape[1])).T > 0.5


def assemble(pair_ref, same_ref, cross_ref, core):
    for low in range(2):
        for ref, side in ((same_ref, core), (cross_ref, 1 - core)):
            for y in range(2):
                pair_ref[:, y, 2 * low + side] = ref[low, y, 0]


def pair_rows(pair_ref, kind, me):
    width = pair_ref.shape[-1]
    return [pair_ref[kind, y].reshape(HEAD_SIZE, width) for y in (me, 1 - me)]


def pair_scratch(weights):
    _, _, _, kinds, rows, width = weights[0].shape
    return pltpu.VMEM((kinds, 2, 4, rows, width), jnp.bfloat16)


def project_back_kernel(
    me_ref, up_ref, kind_ref, same_ref, cross_ref, own_ref, other_ref, pair_ref
):
    count, step, width = up_ref.shape
    me = me_ref[0]
    upstream = up_ref[...].reshape(count * step, width)

    @pl.when(pl.program_id(0) == 0)
    def _():
        assemble(pair_ref, same_ref, cross_ref, me_ref[1])

    text = mm(upstream, jnp.concatenate(pair_rows(pair_ref, 0, me), axis=0), NT)
    image = mm(upstream, jnp.concatenate(pair_rows(pair_ref, 1, me), axis=0), NT)
    for b in range(count):
        mask = is_image(kind_ref, me, b)
        rows = slice(b * step, (b + 1) * step)
        for y, ref in enumerate((own_ref, other_ref)):
            at = slice(y * HEAD_SIZE, (y + 1) * HEAD_SIZE)
            ref[b] = jnp.where(mask, image[rows, at], text[rows, at]).astype(jnp.bfloat16)


def project_back(me, upstream, kinds, weights, group=4):
    count, step, width = upstream.shape
    half = pl.BlockSpec((group, step, HEAD_SIZE), lambda g: (g, 0, 0))
    return pl.pallas_call(
        project_back_kernel,
        grid=(count // group,),
        out_shape=[jax.ShapeDtypeStruct((count, step, HEAD_SIZE), jnp.bfloat16)] * 2,
        in_specs=[
            pl.BlockSpec(memory_space=pltpu.SMEM),
            pl.BlockSpec((group, step, width), lambda g: (g, 0, 0)),
            kind_spec(step),
            pl.BlockSpec(memory_space=pltpu.VMEM),
            pl.BlockSpec(memory_space=pltpu.VMEM),
        ],
        out_specs=[half] * 2,
        scratch_shapes=[pair_scratch(weights)],
        compiler_params=pltpu.CompilerParams(vmem_limit_bytes=VMEM_LIMIT),
        cost_estimate=pl.CostEstimate(
            flops=4 * count * step * weights[0].size, bytes_accessed=2 * upstream.size, transcendentals=0
        ),
        name="project_back",
    )(me, upstream, kinds, *weights)


def project_kernel(me_ref, attn_ref, kind_ref, same_ref, cross_ref, out_ref, quad_ref):
    heads, count, step, _ = attn_ref.shape
    width = quad_ref.shape[-1]
    me, core, far = me_ref[0], me_ref[1], me_ref[2]

    @pl.when(pl.program_id(0) == 0)
    def _():
        for low in range(2):
            for ref, side in ((same_ref, core), (cross_ref, 1 - core)):
                for head in range(4):
                    pair = jnp.bitwise_xor(far, head % 2)
                    quad_ref[:, head, 2 * low + side] = ref[low, head // 2, pair]

    rows = []
    for b in range(count):
        kind = kind_ref[b // 2, me, far, b % 2].astype(jnp.float32)[0:1]
        mask = jnp.broadcast_to(kind, (step, step)).T > 0.5
        parts = [attn_ref[h, b].astype(jnp.float32) for h in range(heads)]
        masked = [jnp.where(mask, 0.0, p) for p in parts] + [jnp.where(mask, p, 0.0) for p in parts]
        rows.append(jnp.concatenate(masked, axis=1))
    left = jnp.concatenate(rows, axis=0).astype(jnp.bfloat16)
    right = [quad_ref[k, h].reshape(HEAD_SIZE, width) for k in range(2) for h in range(heads)]
    out_ref[...] = mm(left, jnp.concatenate(right, axis=0)).astype(out_ref.dtype)


def project(me, attn, kinds, weights, group=4):
    heads, count, step, _ = attn.shape
    _, _, _, sides, rows, width = weights[0].shape
    tall = 3 * step // KIND_ROWS
    return pl.pallas_call(
        project_kernel,
        grid=(count // group,),
        out_shape=jax.ShapeDtypeStruct((count * step, width), jnp.bfloat16),
        in_specs=[
            pl.BlockSpec(memory_space=pltpu.SMEM),
            pl.BlockSpec((heads, group, step, HEAD_SIZE), lambda g: (0, g, 0, 0)),
            pl.BlockSpec((2, 2, 2, 2, KIND_ROWS, HEAD_SIZE), lambda g: (g, 0, 0, 0, tall, 0)),
            pl.BlockSpec(memory_space=pltpu.VMEM),
            pl.BlockSpec(memory_space=pltpu.VMEM),
        ],
        out_specs=pl.BlockSpec((group * step, width), lambda g: (g, 0)),
        scratch_shapes=[pltpu.VMEM((sides, heads, 4, rows, width), jnp.bfloat16)],
        compiler_params=pltpu.CompilerParams(vmem_limit_bytes=VMEM_LIMIT),
        cost_estimate=pl.CostEstimate(
            flops=4 * count * step * weights[0].size,
            bytes_accessed=2 * count * step * width,
            transcendentals=0,
        ),
        name="project",
    )(me, attn, kinds, *weights)


FSDP = ("low", "core")
CTX = ("z", "yh", "xh", "xl")


def exchange(blocks, axis):
    return lax.all_to_all(blocks, axis, split_axis=0, concat_axis=0, tiled=True)


def per_device(query_proj, key_proj, value_proj, modality, out_weight, grad_projected):
    step = query_proj.shape[1]
    axes = ("yh", "core", "xh")
    me = jnp.stack([lax.axis_index(axis) for axis in axes]).astype(jnp.int32)
    partner = [(0, 1), (1, 0)]

    def moved(far):
        return [(f * 4 + x, x * 4 + (f ^ far)) for f in range(4) for x in range(4)]

    upstream = lax.all_gather(grad_projected[0], ("z", "xh", "xl"), axis=0)
    shards = [lax.ppermute(out_weight, (*FSDP, "xh", "xl"), moved(far)) for far in (0, 2)]
    shard = jnp.broadcast_to(jnp.stack(shards), (4, 2, *out_weight.shape))
    packed = pack_heads((query_proj[0], key_proj[0], value_proj[0]), modality)
    qkv = exchange(packed.reshape(32, *packed.shape[3:]), CTX)
    kinds = qkv.reshape(packed.shape)
    shard, qkv = lax.optimization_barrier((shard, qkv))
    same = exchange(shard, ("low", "yh")).reshape(2, 2, *shard.shape[1:])

    attention, sent, lse = attend_forward(qkv, FWD_ROWS)
    same, sent = lax.optimization_barrier((same, sent))
    weights = same, lax.ppermute(same, "core", partner)
    heads = exchange(sent, ("yh", "xh"))
    partial = project(me, heads, kinds.reshape(4, 2, 2, 2, *kinds.shape[3:]), weights)
    projected = lax.psum_scatter(partial, ("z", "xl"), scatter_dimension=0, tiled=True)
    upstream, partial = lax.optimization_barrier((upstream, partial))
    grad_own, grad_other = project_back(me, upstream, kinds, weights)
    grad_other = lax.ppermute(grad_other, "yh", partner)

    grads = attend_backward(me, qkv, attention, lse, grad_own, grad_other)
    grads = exchange(grads, CTX).reshape(4, 2, 4, *grads.shape[1:])
    grad_query, grad_key, grad_value = unpack_heads(grads)
    return projected[None], grad_query[None], grad_key[None], grad_value[None]


def solution(mesh):
    grid = jax.sharding.Mesh(mesh.devices.reshape(2, 2, 4, 2, 2, 2), ("low", "core", *CTX))
    rows = P(FSDP, CTX, None)
    placed = (rows, rows, rows, P(FSDP, CTX), P(None, (*FSDP, *CTX), None), rows)
    return jax.shard_map(
        per_device,
        mesh=grid,
        in_specs=placed,
        out_specs=(rows,) * 4,
        check_vma=False,
    )
```

```python
import functools, math
import jax, jax.numpy as jnp
from jax import lax
from jax.experimental import pallas as pl
from jax.experimental.pallas import tpu as pltpu
from jax.sharding import PartitionSpec as P

HEAD_SIZE = 128
LOG2E = math.log2(math.e)
NT = (((1,), (1,)), ((), ()))
TN = (((0,), (0,)), ((), ()))
VMEM_LIMIT = 56 * 1024 * 1024
FWD_ROWS = 1024
BWD_ROWS = 1024
BWD_VMEM_LIMIT = 36 * 1024 * 1024
KIND_ROWS = 16
PACK = 4


def mm(a, b, dims=(((1,), (0,)), ((), ()))):
    return lax.dot_general(a, b, dims, preferred_element_type=jnp.float32)


def visible(shape, key_dim, shift):
    keys = lax.broadcasted_iota(jnp.int32, shape, key_dim)
    return keys + shift <= lax.broadcasted_iota(jnp.int32, shape, 1 - key_dim)


def fwd_kernel(
    me_ref, qkv_ref, out_ref, own_ref, other_ref, lse_ref, even_ref, odd_ref, total_ref, acc_ref, *, rows
):
    blocks = qkv_ref.shape[0]
    step = HEAD_SIZE
    per = rows // step
    count = blocks // per
    half = rows // 2
    factor = HEAD_SIZE**-0.5 * LOG2E
    stores = (even_ref, odd_ref)

    def get(which, first, size):
        part = qkv_ref[pl.ds(first, size // step), which * step : (which + 1) * step]
        return part.reshape(size, HEAD_SIZE)

    def fold(op, start, s):
        for c in range(0, s.shape[1], HEAD_SIZE):
            start = op(start, s[:, c : c + HEAD_SIZE])
        return start

    def scores(i, j, top):
        s = mm(get(0, i * per, rows), get(1, j * per, rows), NT) * factor
        stores[i % 2][j] = s
        return fold(jnp.maximum, top, s)

    def values(i, j, high):
        p = jnp.exp2(stores[i % 2][j] - high)
        total_ref[...] = fold(jnp.add, total_ref[...], p)
        acc_ref[...] += mm(p.astype(jnp.bfloat16), get(2, j * per, rows))

    def last_scores(i, top):
        highs = []
        for part in range(2):
            size = half * (part + 1)
            at = slice(part * half, (part + 1) * half)
            s = mm(get(0, i * per + part * per // 2, half), get(1, i * per, size), NT) * factor
            s = jnp.where(visible(s.shape, 1, -part * half), s, -jnp.inf)
            stores[i % 2][i, at, :size] = s
            highs.append(jnp.max(fold(jnp.maximum, top[at], s), axis=1, keepdims=True))
        return highs

    def last_values(i, highs):
        for part in range(2):
            size = half * (part + 1)
            at = slice(part * half, (part + 1) * half)
            p = jnp.exp2(stores[i % 2][i, at, :size] - highs[part])
            total = jnp.sum(fold(jnp.add, total_ref[at], p), axis=1, keepdims=True)
            acc = acc_ref[at] + mm(p.astype(jnp.bfloat16), get(2, i * per, size))
            out = (acc / total).astype(jnp.bfloat16)
            first = i * per + part * per // 2
            out_ref[first : first + per // 2] = out.reshape(-1, step, HEAD_SIZE)
            lse = jnp.broadcast_to(highs[part] + jnp.log2(total), (half, HEAD_SIZE))
            lse_ref[i, :, at] = lse.T[0:1]

    low = jnp.full((rows, HEAD_SIZE), -jnp.inf, jnp.float32)
    highs = last_scores(0, low)
    for i in range(count):
        total_ref[...] = jnp.zeros_like(total_ref)
        acc_ref[...] = jnp.zeros_like(acc_ref)
        high = jnp.concatenate(highs, axis=0)
        top = low

        def both(j, top):
            values(i, j, high)
            return scores(i + 1, j, top) if i + 1 < count else top

        top = lax.fori_loop(0, i, both, top)
        if i + 1 < count:
            top = scores(i + 1, i, top)
        last_values(i, highs)
        if i + 1 < count:
            highs = last_scores(i + 1, top)
    me = me_ref[0]
    half = blocks // 8
    for z in range(4):
        own_ref[z * half : (z + 1) * half] = out_ref[pl.ds((2 * z + me) * half, half)]
        other_ref[z * half : (z + 1) * half] = out_ref[pl.ds((2 * z + 1 - me) * half, half)]


def attend_forward(me, qkv, rows):
    blocks, step = qkv.shape[0], HEAD_SIZE
    length = blocks * step
    return pl.pallas_call(
        functools.partial(fwd_kernel, rows=rows),
        out_shape=(
            jax.ShapeDtypeStruct((blocks, step, HEAD_SIZE), jnp.bfloat16),
            jax.ShapeDtypeStruct((blocks // 2, step, HEAD_SIZE), jnp.bfloat16),
            jax.ShapeDtypeStruct((blocks // 2, step, HEAD_SIZE), jnp.bfloat16),
            jax.ShapeDtypeStruct((length // rows, 1, rows), jnp.float32),
        ),
        in_specs=[
            pl.BlockSpec(memory_space=pltpu.SMEM),
            pl.BlockSpec(memory_space=pltpu.VMEM),
        ],
        out_specs=[pl.BlockSpec(memory_space=pltpu.VMEM)] * 4,
        scratch_shapes=[
            pltpu.VMEM((length // rows - 1, rows, rows), jnp.float32),
            pltpu.VMEM((length // rows, rows, rows), jnp.float32),
        ]
        + [pltpu.VMEM((rows, HEAD_SIZE), jnp.float32)] * 2,
        compiler_params=pltpu.CompilerParams(vmem_limit_bytes=VMEM_LIMIT),
        cost_estimate=pl.CostEstimate(
            flops=12 * length * length * HEAD_SIZE,
            bytes_accessed=8 * length * HEAD_SIZE,
            transcendentals=length * length // 2,
        ),
        name="attend_forward",
    )(me, qkv)


def bwd_half(y, qkv_ref, out_ref, lse_ref, grad_ref, dq_ref, dk_ref, dv_ref, write, *, rows):
    blocks = qkv_ref.shape[0]
    step = HEAD_SIZE
    per = rows // step
    half = per // 2
    width = rows // 2
    scale = HEAD_SIZE**-0.5
    factor = scale * LOG2E

    def get(which, first, size):
        part = qkv_ref[pl.ds(first, size // step), which * step : (which + 1) * step]
        return part.reshape(size, HEAD_SIZE)

    def query_block(z, _):
        first = z * per + y * half
        query = get(0, first, width)
        grad = grad_ref[pl.ds(z * half, half)].reshape(width, HEAD_SIZE)
        attn = out_ref[pl.ds(first, half)].reshape(width, HEAD_SIZE)
        prod = grad.astype(jnp.float32) * attn.astype(jnp.float32)
        delta = jnp.sum(prod.T, axis=0, keepdims=True)
        lse = lse_ref[2 * z + y]
        dq_ref[...] = jnp.zeros_like(dq_ref)

        def key_block(j, size, shift=None):
            key = get(1, j * per, size)
            to = pl.ds(j * rows, size)
            p = jnp.exp2(mm(key, query, NT) * factor - lse)
            if shift is not None:
                p = jnp.where(visible(p.shape, 0, shift), p, 0.0)
            dv_ref[to] += mm(p.astype(jnp.bfloat16), grad)
            ds = (p * (mm(get(2, j * per, size), grad, NT) - delta) * scale).astype(jnp.bfloat16)
            dk_ref[to] += mm(ds, query)
            dq_ref[...] += mm(ds, key, TN)

        def body(j, _):
            key_block(j, rows)
            return 0

        lax.fori_loop(0, z, body, 0)

        @pl.when(y == 0)
        def _():
            key_block(z, width, 0)

        @pl.when(y == 1)
        def _():
            key_block(z, rows, -width)

        write(z, first, dq_ref[...].astype(jnp.bfloat16).reshape(half, step, HEAD_SIZE))
        return 0

    lax.fori_loop(0, blocks // per, query_block, 0)


def bwd_first_kernel(
    me_ref, qkv_ref, out_ref, lse_ref, grad_ref, done_ref, dk_ref, dv_ref, dq_ref, *, rows
):
    dk_ref[...] = jnp.zeros_like(dk_ref)
    dv_ref[...] = jnp.zeros_like(dv_ref)
    half = rows // HEAD_SIZE // 2

    def write(z, first, value):
        done_ref[pl.ds(z * half, half)] = value

    bwd_half(me_ref[0], qkv_ref, out_ref, lse_ref, grad_ref, dq_ref, dk_ref, dv_ref, write, rows=rows)


def bwd_second_kernel(
    me_ref, qkv_ref, out_ref, lse_ref, grad_ref, done_ref, dk_ref, dv_ref, res_ref, dq_ref, *, rows
):
    blocks = qkv_ref.shape[0]
    per = rows // HEAD_SIZE
    half = per // 2
    me = me_ref[0]
    for z in range(blocks // per):
        res_ref[pl.ds(z * per + me * half, half), 0] = done_ref[z * half : (z + 1) * half]

    def write(z, first, value):
        res_ref[pl.ds(first, half), 0] = value

    bwd_half(1 - me, qkv_ref, out_ref, lse_ref, grad_ref, dq_ref, dk_ref, dv_ref, write, rows=rows)
    res_ref[:, 1] = dk_ref[...].astype(jnp.bfloat16).reshape(blocks, HEAD_SIZE, HEAD_SIZE)
    res_ref[:, 2] = dv_ref[...].astype(jnp.bfloat16).reshape(blocks, HEAD_SIZE, HEAD_SIZE)


def attend_backward(me, qkv, out, lse, grad_own, grad_other, rows):
    blocks, step = qkv.shape[0], HEAD_SIZE
    length = blocks * step
    lse = lse.reshape(2 * length // rows, 1, rows // 2)
    vmem = pl.BlockSpec(memory_space=pltpu.VMEM)
    common = dict(
        scratch_shapes=[pltpu.VMEM((rows // 2, HEAD_SIZE), jnp.float32)],
        compiler_params=pltpu.CompilerParams(vmem_limit_bytes=BWD_VMEM_LIMIT),
        cost_estimate=pl.CostEstimate(
            flops=10 * length * length * HEAD_SIZE,
            bytes_accessed=16 * length * HEAD_SIZE,
            transcendentals=length * length // 4,
        ),
    )
    sums = jax.ShapeDtypeStruct((length, HEAD_SIZE), jnp.float32)
    done, dk, dv = pl.pallas_call(
        functools.partial(bwd_first_kernel, rows=rows),
        out_shape=[jax.ShapeDtypeStruct((blocks // 2, step, HEAD_SIZE), jnp.bfloat16), sums, sums],
        in_specs=[pl.BlockSpec(memory_space=pltpu.SMEM)] + [vmem] * 4,
        out_specs=[vmem] * 3,
        name="backward_own",
        **common,
    )(me, qkv, out, lse, grad_own)
    return pl.pallas_call(
        functools.partial(bwd_second_kernel, rows=rows),
        out_shape=jax.ShapeDtypeStruct((blocks, 3, step, HEAD_SIZE), jnp.bfloat16),
        in_specs=[pl.BlockSpec(memory_space=pltpu.SMEM)] + [vmem] * 7,
        out_specs=vmem,
        name="backward_other",
        **common,
    )(me, qkv, out, lse, grad_other, done, dk, dv)


def pack_kernel(q_ref, k_ref, v_ref, kind_ref, out_ref):
    step = q_ref.shape[0]
    kind = jnp.broadcast_to(kind_ref[...].astype(jnp.float32), (KIND_ROWS, HEAD_SIZE))
    for h in range(2 * PACK):
        at = slice(h * HEAD_SIZE, (h + 1) * HEAD_SIZE)
        for w, ref in enumerate((q_ref, k_ref, v_ref)):
            out_ref[h // 2, h % 2, 0, w * step : (w + 1) * step] = ref[:, at]
        out_ref[h // 2, h % 2, 0, 3 * step :] = kind.astype(jnp.bfloat16)


def owner(*tail):
    per = 4 // PACK
    return pl.BlockSpec(
        (PACK, 2, 1, *tail), lambda g: (g % per, 0, g // per, *([0] * len(tail)))
    )


def pack_heads(arrays, kind):
    step, width = arrays[0].shape
    flat = pl.BlockSpec((step, 2 * PACK * HEAD_SIZE), lambda g: (0, g))
    tall = 3 * step + KIND_ROWS
    return pl.pallas_call(
        pack_kernel,
        grid=(16 // PACK,),
        out_shape=jax.ShapeDtypeStruct((4, 2, 4, tall, HEAD_SIZE), jnp.bfloat16),
        in_specs=[flat] * 3 + [pl.BlockSpec((1, step), lambda g: (0, 0))],
        out_specs=owner(tall, HEAD_SIZE),
        name="pack_heads",
    )(*arrays, kind)


def unpack_kernel(in_ref, q_ref, k_ref, v_ref):
    for h in range(2 * PACK):
        at = slice(h * HEAD_SIZE, (h + 1) * HEAD_SIZE)
        for w, ref in enumerate((q_ref, k_ref, v_ref)):
            ref[:, at] = in_ref[h // 2, h % 2, 0, w]


def unpack_heads(stacked):
    step = stacked.shape[-2]
    flat = pl.BlockSpec((step, 2 * PACK * HEAD_SIZE), lambda g: (0, g))
    return pl.pallas_call(
        unpack_kernel,
        grid=(16 // PACK,),
        out_shape=[jax.ShapeDtypeStruct((step, 32 * HEAD_SIZE), jnp.bfloat16)] * 3,
        in_specs=[owner(3, step, HEAD_SIZE)],
        out_specs=[flat] * 3,
        name="unpack_heads",
    )(stacked)


def kind_spec(step):
    return pl.BlockSpec((1, 2, 4, KIND_ROWS, HEAD_SIZE), lambda g: (g, 0, 0, 3 * step // KIND_ROWS, 0))


def is_image(kind_ref, me, b):
    row = kind_ref[0, me, b].astype(jnp.float32)[0:1]
    return jnp.broadcast_to(row, (row.shape[1], row.shape[1])).T > 0.5


def assemble(pair_ref, same_ref, cross_ref, core):
    for low in range(2):
        for ref, side in ((same_ref, core), (cross_ref, 1 - core)):
            for y in range(2):
                pair_ref[:, y, 2 * low + side] = ref[low, y]


def pair_rows(pair_ref, kind, me):
    width = pair_ref.shape[-1]
    return [pair_ref[kind, y].reshape(HEAD_SIZE, width) for y in (me, 1 - me)]


def pair_scratch(weights):
    _, _, kinds, rows, width = weights[0].shape
    return pltpu.VMEM((kinds, 2, 4, rows, width), jnp.bfloat16)


def project_back_kernel(
    me_ref, up_ref, kind_ref, same_ref, cross_ref, own_ref, other_ref, pair_ref
):
    count, step, width = up_ref.shape
    me = me_ref[0]
    upstream = up_ref[...].reshape(count * step, width)

    @pl.when(pl.program_id(0) == 0)
    def _():
        assemble(pair_ref, same_ref, cross_ref, me_ref[1])

    text = mm(upstream, jnp.concatenate(pair_rows(pair_ref, 0, me), axis=0), NT)
    image = mm(upstream, jnp.concatenate(pair_rows(pair_ref, 1, me), axis=0), NT)
    for b in range(count):
        mask = is_image(kind_ref, me, b)
        rows = slice(b * step, (b + 1) * step)
        for y, ref in enumerate((own_ref, other_ref)):
            at = slice(y * HEAD_SIZE, (y + 1) * HEAD_SIZE)
            ref[b] = jnp.where(mask, image[rows, at], text[rows, at]).astype(jnp.bfloat16)


def project_back(me, upstream, kinds, weights, group=4):
    count, step, width = upstream.shape
    half = pl.BlockSpec((group, step, HEAD_SIZE), lambda g: (g, 0, 0))
    return pl.pallas_call(
        project_back_kernel,
        grid=(count // group,),
        out_shape=[jax.ShapeDtypeStruct((count, step, HEAD_SIZE), jnp.bfloat16)] * 2,
        in_specs=[
            pl.BlockSpec(memory_space=pltpu.SMEM),
            pl.BlockSpec((group, step, width), lambda g: (g, 0, 0)),
            kind_spec(step),
            pl.BlockSpec(memory_space=pltpu.VMEM),
            pl.BlockSpec(memory_space=pltpu.VMEM),
        ],
        out_specs=[half] * 2,
        scratch_shapes=[pair_scratch(weights)],
        compiler_params=pltpu.CompilerParams(vmem_limit_bytes=VMEM_LIMIT),
        cost_estimate=pl.CostEstimate(
            flops=4 * count * step * weights[0].size, bytes_accessed=2 * upstream.size, transcendentals=0
        ),
        name="project_back",
    )(me, upstream, kinds, *weights)


def project_kernel(
    me_ref, own_ref, other_ref, kind_ref, same_ref, cross_ref, out_ref, pair_ref
):
    count, step, _ = own_ref.shape
    me = me_ref[0]
    rows = []
    for b in range(count):
        mask = is_image(kind_ref, me, b)
        parts = [ref[b].astype(jnp.float32) for ref in (own_ref, other_ref)]
        masked = [jnp.where(mask, 0.0, p) for p in parts] + [jnp.where(mask, p, 0.0) for p in parts]
        rows.append(jnp.concatenate(masked, axis=1))
    left = jnp.concatenate(rows, axis=0).astype(jnp.bfloat16)

    @pl.when(pl.program_id(0) == 0)
    def _():
        assemble(pair_ref, same_ref, cross_ref, me_ref[1])

    right = jnp.concatenate(pair_rows(pair_ref, 0, me) + pair_rows(pair_ref, 1, me), axis=0)
    out_ref[...] = mm(left, right).astype(out_ref.dtype)


def project(me, own, other, kinds, weights, group=4):
    count, step, _ = own.shape
    width = weights[0].shape[-1]
    half = pl.BlockSpec((group, step, HEAD_SIZE), lambda g: (g, 0, 0))
    return pl.pallas_call(
        project_kernel,
        grid=(count // group,),
        out_shape=jax.ShapeDtypeStruct((count * step, width), jnp.bfloat16),
        in_specs=[
            pl.BlockSpec(memory_space=pltpu.SMEM),
            half,
            half,
            kind_spec(step),
            pl.BlockSpec(memory_space=pltpu.VMEM),
            pl.BlockSpec(memory_space=pltpu.VMEM),
        ],
        out_specs=pl.BlockSpec((group * step, width), lambda g: (g, 0)),
        scratch_shapes=[pair_scratch(weights)],
        compiler_params=pltpu.CompilerParams(vmem_limit_bytes=VMEM_LIMIT),
        cost_estimate=pl.CostEstimate(
            flops=4 * count * step * weights[0].size,
            bytes_accessed=2 * count * step * width,
            transcendentals=0,
        ),
        name="project",
    )(me, own, other, kinds, *weights)


FSDP = ("low", "core")
CTX = ("z", "yh", "x")


def exchange(blocks, axis):
    return lax.all_to_all(blocks, axis, split_axis=0, concat_axis=0, tiled=True)


def per_device(query_proj, key_proj, value_proj, modality, out_weight, grad_projected):
    step = query_proj.shape[1]
    me = jnp.stack([lax.axis_index("yh"), lax.axis_index("core")]).astype(jnp.int32)
    partner = [(0, 1), (1, 0)]
    swap = [(f * 4 + x, x * 4 + f) for f in range(4) for x in range(4)]

    upstream = lax.all_gather(grad_projected[0], ("z", "x"), axis=0)
    shard = lax.ppermute(out_weight, ("low", "core", "x"), swap)
    shard = jnp.broadcast_to(shard, (4, *shard.shape))
    packed = pack_heads((query_proj[0], key_proj[0], value_proj[0]), modality)
    qkv = exchange(packed.reshape(32, *packed.shape[3:]), CTX)
    kinds = qkv.reshape(packed.shape)
    shard, qkv = lax.optimization_barrier((shard, qkv))
    same = exchange(shard, ("low", "yh")).reshape(2, 2, *out_weight.shape)

    attention, own, other, lse = attend_forward(me, qkv, FWD_ROWS)
    same, other = lax.optimization_barrier((same, other))
    weights = same, lax.ppermute(same, "core", partner)
    other = lax.ppermute(other, "yh", partner)
    partial = project(me, own, other, kinds, weights)
    projected = lax.psum_scatter(partial, ("z", "x"), scatter_dimension=0, tiled=True)
    upstream, partial = lax.optimization_barrier((upstream, partial))
    grad_own, grad_other = project_back(me, upstream, kinds, weights)
    grad_other = lax.ppermute(grad_other, "yh", partner)

    grads = attend_backward(me, qkv, attention, lse, grad_own, grad_other, BWD_ROWS)
    grads = exchange(grads, CTX).reshape(4, 2, 4, *grads.shape[1:])
    grad_query, grad_key, grad_value = unpack_heads(grads)
    return projected[None], grad_query[None], grad_key[None], grad_value[None]


def solution(mesh):
    grid = jax.sharding.Mesh(mesh.devices.reshape(2, 2, 4, 2, 4), ("low", "core", *CTX))
    rows = P(FSDP, CTX, None)
    placed = (rows, rows, rows, P(FSDP, CTX), P(None, (*FSDP, *CTX), None), rows)
    return jax.shard_map(
        per_device,
        mesh=grid,
        in_specs=placed,
        out_specs=(rows,) * 4,
        check_vma=False,
    )
```

```python
import functools, math
import jax, jax.numpy as jnp
from jax import lax
from jax.experimental import pallas as pl
from jax.experimental.pallas import tpu as pltpu
from jax.sharding import PartitionSpec as P

HEAD_SIZE = 128
LOG2E = math.log2(math.e)
NT = (((1,), (1,)), ((), ()))
TN = (((0,), (0,)), ((), ()))
VMEM_LIMIT = 56 * 1024 * 1024
FWD_ROWS = 1024
BWD_ROWS = 1024
BWD_VMEM_LIMIT = 36 * 1024 * 1024
KIND_ROWS = 16
PACK = 4


def mm(a, b, dims=(((1,), (0,)), ((), ()))):
    return lax.dot_general(a, b, dims, preferred_element_type=jnp.float32)


def visible(shape, key_dim, shift):
    keys = lax.broadcasted_iota(jnp.int32, shape, key_dim)
    return keys + shift <= lax.broadcasted_iota(jnp.int32, shape, 1 - key_dim)


def fwd_kernel(
    me_ref, qkv_ref, out_ref, own_ref, other_ref, lse_ref, even_ref, odd_ref, total_ref, acc_ref, *, rows
):
    blocks = qkv_ref.shape[0]
    step = HEAD_SIZE
    per = rows // step
    count = blocks // per
    half = rows // 2
    factor = HEAD_SIZE**-0.5 * LOG2E
    stores = (even_ref, odd_ref)

    def get(which, first, size):
        part = qkv_ref[pl.ds(first, size // step), which * step : (which + 1) * step]
        return part.reshape(size, HEAD_SIZE)

    def fold(op, start, s):
        for c in range(0, s.shape[1], HEAD_SIZE):
            start = op(start, s[:, c : c + HEAD_SIZE])
        return start

    def scores(i, j, top):
        s = mm(get(0, i * per, rows), get(1, j * per, rows), NT) * factor
        stores[i % 2][j] = s
        return fold(jnp.maximum, top, s)

    def values(i, j, high):
        p = jnp.exp2(stores[i % 2][j] - high)
        total_ref[...] = fold(jnp.add, total_ref[...], p)
        acc_ref[...] += mm(p.astype(jnp.bfloat16), get(2, j * per, rows))

    def last_scores(i, top):
        highs = []
        for part in range(2):
            size = half * (part + 1)
            at = slice(part * half, (part + 1) * half)
            s = mm(get(0, i * per + part * per // 2, half), get(1, i * per, size), NT) * factor
            s = jnp.where(visible(s.shape, 1, -part * half), s, -jnp.inf)
            stores[i % 2][i, at, :size] = s
            highs.append(jnp.max(fold(jnp.maximum, top[at], s), axis=1, keepdims=True))
        return highs

    def last_values(i, highs):
        for part in range(2):
            size = half * (part + 1)
            at = slice(part * half, (part + 1) * half)
            p = jnp.exp2(stores[i % 2][i, at, :size] - highs[part])
            total = jnp.sum(fold(jnp.add, total_ref[at], p), axis=1, keepdims=True)
            acc = acc_ref[at] + mm(p.astype(jnp.bfloat16), get(2, i * per, size))
            out = (acc / total).astype(jnp.bfloat16)
            first = i * per + part * per // 2
            out_ref[first : first + per // 2] = out.reshape(-1, step, HEAD_SIZE)
            lse = jnp.broadcast_to(highs[part] + jnp.log2(total), (half, HEAD_SIZE))
            lse_ref[i, :, at] = lse.T[0:1]

    low = jnp.full((rows, HEAD_SIZE), -jnp.inf, jnp.float32)
    highs = last_scores(0, low)
    for i in range(count):
        total_ref[...] = jnp.zeros_like(total_ref)
        acc_ref[...] = jnp.zeros_like(acc_ref)
        high = jnp.concatenate(highs, axis=0)
        top = low

        def both(j, top):
            values(i, j, high)
            return scores(i + 1, j, top) if i + 1 < count else top

        top = lax.fori_loop(0, i, both, top)
        if i + 1 < count:
            top = scores(i + 1, i, top)
        last_values(i, highs)
        if i + 1 < count:
            highs = last_scores(i + 1, top)
    me = me_ref[0]
    half = blocks // 8
    for z in range(4):
        own_ref[z * half : (z + 1) * half] = out_ref[pl.ds((2 * z + me) * half, half)]
        other_ref[z * half : (z + 1) * half] = out_ref[pl.ds((2 * z + 1 - me) * half, half)]


def attend_forward(me, qkv, rows):
    blocks, step = qkv.shape[0], HEAD_SIZE
    length = blocks * step
    return pl.pallas_call(
        functools.partial(fwd_kernel, rows=rows),
        out_shape=(
            jax.ShapeDtypeStruct((blocks, step, HEAD_SIZE), jnp.bfloat16),
            jax.ShapeDtypeStruct((blocks // 2, step, HEAD_SIZE), jnp.bfloat16),
            jax.ShapeDtypeStruct((blocks // 2, step, HEAD_SIZE), jnp.bfloat16),
            jax.ShapeDtypeStruct((length // rows, 1, rows), jnp.float32),
        ),
        in_specs=[
            pl.BlockSpec(memory_space=pltpu.SMEM),
            pl.BlockSpec(memory_space=pltpu.VMEM),
        ],
        out_specs=[pl.BlockSpec(memory_space=pltpu.VMEM)] * 4,
        scratch_shapes=[
            pltpu.VMEM((length // rows - 1, rows, rows), jnp.float32),
            pltpu.VMEM((length // rows, rows, rows), jnp.float32),
        ]
        + [pltpu.VMEM((rows, HEAD_SIZE), jnp.float32)] * 2,
        compiler_params=pltpu.CompilerParams(vmem_limit_bytes=VMEM_LIMIT),
        cost_estimate=pl.CostEstimate(
            flops=12 * length * length * HEAD_SIZE,
            bytes_accessed=8 * length * HEAD_SIZE,
            transcendentals=length * length // 2,
        ),
        name="attend_forward",
    )(me, qkv)


def bwd_half(y, qkv_ref, out_ref, lse_ref, grad_ref, dq_ref, dk_ref, dv_ref, write, *, rows):
    blocks = qkv_ref.shape[0]
    step = HEAD_SIZE
    per = rows // step
    half = per // 2
    width = rows // 2
    scale = HEAD_SIZE**-0.5
    factor = scale * LOG2E

    def get(which, first, size):
        part = qkv_ref[pl.ds(first, size // step), which * step : (which + 1) * step]
        return part.reshape(size, HEAD_SIZE)

    def query_block(z, _):
        first = z * per + y * half
        query = get(0, first, width)
        grad = grad_ref[pl.ds(z * half, half)].reshape(width, HEAD_SIZE)
        attn = out_ref[pl.ds(first, half)].reshape(width, HEAD_SIZE)
        prod = grad.astype(jnp.float32) * attn.astype(jnp.float32)
        delta = jnp.sum(prod.T, axis=0, keepdims=True)
        lse = lse_ref[2 * z + y]
        dq_ref[...] = jnp.zeros_like(dq_ref)

        def key_block(j, size, shift=None):
            key = get(1, j * per, size)
            to = pl.ds(j * rows, size)
            p = jnp.exp2(mm(key, query, NT) * factor - lse)
            if shift is not None:
                p = jnp.where(visible(p.shape, 0, shift), p, 0.0)
            dv_ref[to] += mm(p.astype(jnp.bfloat16), grad)
            ds = (p * (mm(get(2, j * per, size), grad, NT) - delta) * scale).astype(jnp.bfloat16)
            dk_ref[to] += mm(ds, query)
            dq_ref[...] += mm(ds, key, TN)

        def body(j, _):
            key_block(j, rows)
            return 0

        lax.fori_loop(0, z, body, 0)

        @pl.when(y == 0)
        def _():
            key_block(z, width, 0)

        @pl.when(y == 1)
        def _():
            key_block(z, rows, -width)

        write(z, first, dq_ref[...].astype(jnp.bfloat16).reshape(half, step, HEAD_SIZE))
        return 0

    lax.fori_loop(0, blocks // per, query_block, 0)


def bwd_first_kernel(
    me_ref, qkv_ref, out_ref, lse_ref, grad_ref, done_ref, dk_ref, dv_ref, dq_ref, *, rows
):
    dk_ref[...] = jnp.zeros_like(dk_ref)
    dv_ref[...] = jnp.zeros_like(dv_ref)
    half = rows // HEAD_SIZE // 2

    def write(z, first, value):
        done_ref[pl.ds(z * half, half)] = value

    bwd_half(me_ref[0], qkv_ref, out_ref, lse_ref, grad_ref, dq_ref, dk_ref, dv_ref, write, rows=rows)


def bwd_second_kernel(
    me_ref, qkv_ref, out_ref, lse_ref, grad_ref, done_ref, dk_ref, dv_ref, res_ref, dq_ref, *, rows
):
    blocks = qkv_ref.shape[0]
    per = rows // HEAD_SIZE
    half = per // 2
    me = me_ref[0]
    for z in range(blocks // per):
        res_ref[pl.ds(z * per + me * half, half), 0] = done_ref[z * half : (z + 1) * half]

    def write(z, first, value):
        res_ref[pl.ds(first, half), 0] = value

    bwd_half(1 - me, qkv_ref, out_ref, lse_ref, grad_ref, dq_ref, dk_ref, dv_ref, write, rows=rows)
    res_ref[:, 1] = dk_ref[...].astype(jnp.bfloat16).reshape(blocks, HEAD_SIZE, HEAD_SIZE)
    res_ref[:, 2] = dv_ref[...].astype(jnp.bfloat16).reshape(blocks, HEAD_SIZE, HEAD_SIZE)


def attend_backward(me, qkv, out, lse, grad_own, grad_other, rows):
    blocks, step = qkv.shape[0], HEAD_SIZE
    length = blocks * step
    lse = lse.reshape(2 * length // rows, 1, rows // 2)
    vmem = pl.BlockSpec(memory_space=pltpu.VMEM)
    common = dict(
        scratch_shapes=[pltpu.VMEM((rows // 2, HEAD_SIZE), jnp.float32)],
        compiler_params=pltpu.CompilerParams(vmem_limit_bytes=BWD_VMEM_LIMIT),
        cost_estimate=pl.CostEstimate(
            flops=10 * length * length * HEAD_SIZE,
            bytes_accessed=16 * length * HEAD_SIZE,
            transcendentals=length * length // 4,
        ),
    )
    sums = jax.ShapeDtypeStruct((length, HEAD_SIZE), jnp.float32)
    done, dk, dv = pl.pallas_call(
        functools.partial(bwd_first_kernel, rows=rows),
        out_shape=[jax.ShapeDtypeStruct((blocks // 2, step, HEAD_SIZE), jnp.bfloat16), sums, sums],
        in_specs=[pl.BlockSpec(memory_space=pltpu.SMEM)] + [vmem] * 4,
        out_specs=[vmem] * 3,
        name="backward_own",
        **common,
    )(me, qkv, out, lse, grad_own)
    return pl.pallas_call(
        functools.partial(bwd_second_kernel, rows=rows),
        out_shape=jax.ShapeDtypeStruct((blocks, 3, step, HEAD_SIZE), jnp.bfloat16),
        in_specs=[pl.BlockSpec(memory_space=pltpu.SMEM)] + [vmem] * 7,
        out_specs=vmem,
        name="backward_other",
        **common,
    )(me, qkv, out, lse, grad_other, done, dk, dv)


def pack_kernel(q_ref, k_ref, v_ref, kind_ref, out_ref):
    step = q_ref.shape[0]
    kind = jnp.broadcast_to(kind_ref[...].astype(jnp.float32), (KIND_ROWS, HEAD_SIZE))
    for h in range(2 * PACK):
        at = slice(h * HEAD_SIZE, (h + 1) * HEAD_SIZE)
        for w, ref in enumerate((q_ref, k_ref, v_ref)):
            out_ref[h // 2, h % 2, 0, w * step : (w + 1) * step] = ref[:, at]
        out_ref[h // 2, h % 2, 0, 3 * step :] = kind.astype(jnp.bfloat16)


def owner(*tail):
    per = 4 // PACK
    return pl.BlockSpec(
        (PACK, 2, 1, *tail), lambda g: (g % per, 0, g // per, *([0] * len(tail)))
    )


def pack_heads(arrays, kind):
    step, width = arrays[0].shape
    flat = pl.BlockSpec((step, 2 * PACK * HEAD_SIZE), lambda g: (0, g))
    tall = 3 * step + KIND_ROWS
    return pl.pallas_call(
        pack_kernel,
        grid=(16 // PACK,),
        out_shape=jax.ShapeDtypeStruct((4, 2, 4, tall, HEAD_SIZE), jnp.bfloat16),
        in_specs=[flat] * 3 + [pl.BlockSpec((1, step), lambda g: (0, 0))],
        out_specs=owner(tall, HEAD_SIZE),
        name="pack_heads",
    )(*arrays, kind)


def unpack_kernel(in_ref, q_ref, k_ref, v_ref):
    for h in range(2 * PACK):
        at = slice(h * HEAD_SIZE, (h + 1) * HEAD_SIZE)
        for w, ref in enumerate((q_ref, k_ref, v_ref)):
            ref[:, at] = in_ref[h // 2, h % 2, 0, w]


def unpack_heads(stacked):
    step = stacked.shape[-2]
    flat = pl.BlockSpec((step, 2 * PACK * HEAD_SIZE), lambda g: (0, g))
    return pl.pallas_call(
        unpack_kernel,
        grid=(16 // PACK,),
        out_shape=[jax.ShapeDtypeStruct((step, 32 * HEAD_SIZE), jnp.bfloat16)] * 3,
        in_specs=[owner(3, step, HEAD_SIZE)],
        out_specs=[flat] * 3,
        name="unpack_heads",
    )(stacked)


def kind_spec(step):
    return pl.BlockSpec((1, 2, 4, KIND_ROWS, HEAD_SIZE), lambda g: (g, 0, 0, 3 * step // KIND_ROWS, 0))


def is_image(kind_ref, me, b):
    row = kind_ref[0, me, b].astype(jnp.float32)[0:1]
    return jnp.broadcast_to(row, (row.shape[1], row.shape[1])).T > 0.5


def assemble(pair_ref, same_ref, cross_ref, core):
    for low in range(2):
        for ref, side in ((same_ref, core), (cross_ref, 1 - core)):
            for y in range(2):
                pair_ref[:, y, 2 * low + side] = ref[low, y]


def pair_rows(pair_ref, kind, me):
    width = pair_ref.shape[-1]
    return [pair_ref[kind, y].reshape(HEAD_SIZE, width) for y in (me, 1 - me)]


def pair_scratch(weights):
    _, _, kinds, rows, width = weights[0].shape
    return pltpu.VMEM((kinds, 2, 4, rows, width), jnp.bfloat16)


def project_back_kernel(
    me_ref, up_ref, kind_ref, same_ref, cross_ref, own_ref, other_ref, pair_ref
):
    count, step, width = up_ref.shape
    me = me_ref[0]
    upstream = up_ref[...].reshape(count * step, width)

    @pl.when(pl.program_id(0) == 0)
    def _():
        assemble(pair_ref, same_ref, cross_ref, me_ref[1])

    text = mm(upstream, jnp.concatenate(pair_rows(pair_ref, 0, me), axis=0), NT)
    image = mm(upstream, jnp.concatenate(pair_rows(pair_ref, 1, me), axis=0), NT)
    for b in range(count):
        mask = is_image(kind_ref, me, b)
        rows = slice(b * step, (b + 1) * step)
        for y, ref in enumerate((own_ref, other_ref)):
            at = slice(y * HEAD_SIZE, (y + 1) * HEAD_SIZE)
            ref[b] = jnp.where(mask, image[rows, at], text[rows, at]).astype(jnp.bfloat16)


def project_back(me, upstream, kinds, weights, group=4):
    count, step, width = upstream.shape
    half = pl.BlockSpec((group, step, HEAD_SIZE), lambda g: (g, 0, 0))
    return pl.pallas_call(
        project_back_kernel,
        grid=(count // group,),
        out_shape=[jax.ShapeDtypeStruct((count, step, HEAD_SIZE), jnp.bfloat16)] * 2,
        in_specs=[
            pl.BlockSpec(memory_space=pltpu.SMEM),
            pl.BlockSpec((group, step, width), lambda g: (g, 0, 0)),
            kind_spec(step),
            pl.BlockSpec(memory_space=pltpu.VMEM),
            pl.BlockSpec(memory_space=pltpu.VMEM),
        ],
        out_specs=[half] * 2,
        scratch_shapes=[pair_scratch(weights)],
        compiler_params=pltpu.CompilerParams(vmem_limit_bytes=VMEM_LIMIT),
        cost_estimate=pl.CostEstimate(
            flops=4 * count * step * weights[0].size, bytes_accessed=2 * upstream.size, transcendentals=0
        ),
        name="project_back",
    )(me, upstream, kinds, *weights)


def project_kernel(
    me_ref, own_ref, other_ref, kind_ref, same_ref, cross_ref, out_ref, pair_ref
):
    count, step, _ = own_ref.shape
    me = me_ref[0]
    rows = []
    for b in range(count):
        mask = is_image(kind_ref, me, b)
        parts = [ref[b].astype(jnp.float32) for ref in (own_ref, other_ref)]
        masked = [jnp.where(mask, 0.0, p) for p in parts] + [jnp.where(mask, p, 0.0) for p in parts]
        rows.append(jnp.concatenate(masked, axis=1))
    left = jnp.concatenate(rows, axis=0).astype(jnp.bfloat16)

    @pl.when(pl.program_id(0) == 0)
    def _():
        assemble(pair_ref, same_ref, cross_ref, me_ref[1])

    right = jnp.concatenate(pair_rows(pair_ref, 0, me) + pair_rows(pair_ref, 1, me), axis=0)
    out_ref[...] = mm(left, right).astype(out_ref.dtype)


def project(me, own, other, kinds, weights, group=4):
    count, step, _ = own.shape
    width = weights[0].shape[-1]
    half = pl.BlockSpec((group, step, HEAD_SIZE), lambda g: (g, 0, 0))
    return pl.pallas_call(
        project_kernel,
        grid=(count // group,),
        out_shape=jax.ShapeDtypeStruct((count * step, width), jnp.bfloat16),
        in_specs=[
            pl.BlockSpec(memory_space=pltpu.SMEM),
            half,
            half,
            kind_spec(step),
            pl.BlockSpec(memory_space=pltpu.VMEM),
            pl.BlockSpec(memory_space=pltpu.VMEM),
        ],
        out_specs=pl.BlockSpec((group * step, width), lambda g: (g, 0)),
        scratch_shapes=[pair_scratch(weights)],
        compiler_params=pltpu.CompilerParams(vmem_limit_bytes=VMEM_LIMIT),
        cost_estimate=pl.CostEstimate(
            flops=4 * count * step * weights[0].size,
            bytes_accessed=2 * count * step * width,
            transcendentals=0,
        ),
        name="project",
    )(me, own, other, kinds, *weights)


FSDP = ("low", "core")
CTX = ("z", "yh", "x")


def exchange(blocks, axis):
    return lax.all_to_all(blocks, axis, split_axis=0, concat_axis=0, tiled=True)


def per_device(query_proj, key_proj, value_proj, modality, out_weight, grad_projected):
    step = query_proj.shape[1]
    me = jnp.stack([lax.axis_index("yh"), lax.axis_index("core")]).astype(jnp.int32)
    partner = [(0, 1), (1, 0)]
    swap = [(f * 4 + x, x * 4 + f) for f in range(4) for x in range(4)]

    shard = lax.ppermute(out_weight, ("low", "core", "x"), swap)
    shard = jnp.broadcast_to(shard, (4, *shard.shape))
    packed = pack_heads((query_proj[0], key_proj[0], value_proj[0]), modality)
    packed, upstream = lax.optimization_barrier((packed, grad_projected[0]))
    upstream = lax.all_gather(upstream, ("z", "x"), axis=0)
    qkv = exchange(packed.reshape(32, *packed.shape[3:]), CTX)
    kinds = qkv.reshape(packed.shape)
    shard, qkv = lax.optimization_barrier((shard, qkv))
    same = exchange(shard, ("low", "yh")).reshape(2, 2, *out_weight.shape)

    attention, own, other, lse = attend_forward(me, qkv, FWD_ROWS)
    same, other = lax.optimization_barrier((same, other))
    weights = same, lax.ppermute(same, "core", partner)
    other = lax.ppermute(other, "yh", partner)
    partial = project(me, own, other, kinds, weights)
    projected = lax.psum_scatter(partial, ("z", "x"), scatter_dimension=0, tiled=True)
    upstream, partial = lax.optimization_barrier((upstream, partial))
    grad_own, grad_other = project_back(me, upstream, kinds, weights)
    grad_other = lax.ppermute(grad_other, "yh", partner)

    grads = attend_backward(me, qkv, attention, lse, grad_own, grad_other, BWD_ROWS)
    grads = exchange(grads, CTX).reshape(4, 2, 4, *grads.shape[1:])
    grad_query, grad_key, grad_value = unpack_heads(grads)
    return projected[None], grad_query[None], grad_key[None], grad_value[None]


def solution(mesh):
    grid = jax.sharding.Mesh(mesh.devices.reshape(2, 2, 4, 2, 4), ("low", "core", *CTX))
    rows = P(FSDP, CTX, None)
    placed = (rows, rows, rows, P(FSDP, CTX), P(None, (*FSDP, *CTX), None), rows)
    return jax.shard_map(
        per_device,
        mesh=grid,
        in_specs=placed,
        out_specs=(rows,) * 4,
        check_vma=False,
    )
```
